128 devices in a mesh: dom: 32 (over z, y_lo, x), feat: 4 (over y_hi, core).
Axes of the slice: x: 4, y: 4 (y_hi: 2, y_lo: 2; y = y_hi * 2 + y_lo), z: 4, core: 2. Of those that a mesh axis runs over, the one named last changes fastest.
Arguments:
- items: bfloat16 [8192, 1024], P('dom', 'feat'), may hold values from -6 to 6
- self_ids: int32 [8192], P('dom'), may hold values from 0 to 8191
- neighbor_ids: int32 [8192, 50], P('dom'), may hold values from 0 to 8191
- visit_counts: int32 [8192, 50], P('dom'), may hold values from 1 to 63
- w_self: bfloat16 [1024, 1024], P('feat'), may hold values from -0.1875 to 0.1875
- w_neighbor: bfloat16 [1024, 1024], P('feat'), may hold values from -0.75 to 0.75
- bias: float32 [1024], replicated, may hold values from -3 to 3
Outputs:
- embedding: float32 [8192, 1024], P('dom', 'feat')
The draws below stay inside these ranges and needn't reach their ends.
All inputs are finite; a program needn't handle non-finite values.
Results may differ from the reference program's by a relative error of at most 0.0018.
Values may be sent and summed in bfloat16 or wider, within the bound.
No kernel may reach another device: no remote copies, remote signals or barrier semaphores. Data moves between devices by JAX's collectives and lax.ppermute only.
A program may use at most 64 MiB of HBM per device.

```python
import jax
import jax.numpy as jnp
from jax import lax

F = 1024
OUT = 1024
NBR = 50
ITEMS = 8192
BATCH = 8192


def set_ends(values, stream_key, low, high):
    longest = values.shape.index(max(values.shape))
    spots = []
    for shift in (0, 1):
        where = [jax.random.randint(jax.random.fold_in(stream_key, axis), (), 0, length) for axis, length in enumerate(values.shape)]
        where[longest] = (where[longest] + shift) % values.shape[longest]
        spots.append(tuple(where))
    return values.at[spots[0]].set(low).at[spots[1]].set(high)


def block_levels(own_key, dims, pieces, smallest, largest):
    factor_of, own = 1.0, jax.random.fold_in(own_key, 6)
    for axis_at, shards_of in pieces:
        steps = jnp.exp(jax.random.uniform(jax.random.fold_in(own, axis_at), (shards_of,), jnp.float32, smallest / len(pieces), largest / len(pieces)))
        factor_of = factor_of * jnp.repeat(steps, dims[axis_at] // shards_of).reshape([-1 if axis == axis_at else 1 for axis in range(len(dims))])
    return factor_of


def bell_draw(stream_key, dims, width, limit, pieces=(), held_as=jnp.bfloat16):
    drawn = width * jax.random.normal(stream_key, dims, jnp.float32)
    if pieces:
        drawn = drawn * block_levels(stream_key, dims, pieces, -0.22, 0.18)
    return jnp.clip(drawn, -limit, limit).astype(held_as)


def setup_inputs(seed: int = 0) -> dict:
    key_of = jax.random.split(jax.random.key(seed), 8)
    return {
        "items": bell_draw(key_of[0], (ITEMS, F), 1.0, 6.0, ((0, 32), (1, 4))),
        "self_ids": set_ends(jax.random.randint(key_of[1], (BATCH,), 0, ITEMS), jax.random.fold_in(key_of[1], 1), 0, ITEMS - 1).astype(jnp.int32),
        "neighbor_ids": set_ends(jax.random.randint(key_of[2], (BATCH, NBR), 0, ITEMS), jax.random.fold_in(key_of[2], 1), 0, ITEMS - 1).astype(jnp.int32),
        "visit_counts": set_ends(jax.random.randint(key_of[3], (BATCH, NBR), 1, 64), jax.random.fold_in(key_of[3], 1), 1, 63).astype(jnp.int32),
        "w_self": bell_draw(key_of[4], (F, OUT), F ** -0.5, 0.1875, ((0, 4),)),
        "w_neighbor": bell_draw(key_of[5], (F, OUT), (F // 16) ** -0.5, 0.75, ((0, 4),)),
        "bias": bell_draw(key_of[6], (OUT,), 0.5, 3.0, (), jnp.float32),
    }


def reference(items, self_ids, neighbor_ids, visit_counts, w_self, w_neighbor, bias):
    own = items[self_ids]
    total = lax.optimization_barrier(jnp.sum(visit_counts.astype(jnp.float32), axis=1))
    block = 512 if BATCH % 512 == 0 else BATCH
    ids_blocks = neighbor_ids.reshape(BATCH // block, block, NBR)
    count_blocks = visit_counts.reshape(BATCH // block, block, NBR)

    def pool(pair):
        ids, counts = pair
        rows = items[ids].astype(jnp.float32)
        return jnp.einsum('bk,bkf->bf', counts.astype(jnp.float32), rows)
    sums = lax.map(pool, (ids_blocks, count_blocks)).reshape(BATCH, F)
    pooled = (sums / total[:, None]).astype(jnp.bfloat16)
    pre = jnp.dot(own, w_self, preferred_element_type=jnp.float32) + jnp.dot(pooled, w_neighbor, preferred_element_type=jnp.float32)
    hidden = jnp.maximum(pre + bias[None, :], 0.0)
    scale = jnp.sqrt(lax.optimization_barrier(jnp.mean(hidden * hidden, axis=1, keepdims=True)) + 1e-06)
    return hidden / scale
```

```python
import jax
import jax.numpy as jnp
from jax import lax
from jax.experimental import pallas as pl
from jax.experimental.pallas import tpu as pltpu
from jax.sharding import Mesh
from jax.sharding import PartitionSpec as P


DOM = ("z", "yl", "x")
LANES = 128
SLOTS = 64
GROUP = 16
SCALE = 16.0


def shifted(value, axis, step):
    n = lax.axis_size(axis)
    return lax.ppermute(value, axis, [(i, (i + step) % n) for i in range(n)])


def count_kernel(hi_ref, lo_ref, count_ref, self_ref, *rest):
    out_refs, stage = rest[:-1], rest[-1]
    nodes = out_refs[0].shape[0] // 2
    per_out = out_refs[0].shape[1] // LANES
    row = lax.broadcasted_iota(jnp.int32, (LANES, LANES), 0)
    lane = lax.broadcasted_iota(jnp.int32, (GROUP, LANES), 1)

    @pl.loop(0, nodes // GROUP)
    def _(g):
        first = pl.multiple_of(g * GROUP, GROUP)
        first_pair = pl.multiple_of(g * (GROUP // 2), GROUP // 2)
        his = hi_ref[pl.ds(first_pair, GROUP // 2), :]
        los = lo_ref[pl.ds(first_pair, GROUP // 2), :]
        counts = count_ref[pl.ds(first_pair, GROUP // 2), :]
        for p in range(GROUP // 2):
            a = jnp.where(his[p : p + 1, :] == row, counts[p : p + 1, :], 0.0)
            b = jnp.where(los[p : p + 1, :] == row, 1.0, 0.0)
            c = lax.dot_general(
                a.astype(jnp.bfloat16),
                b.astype(jnp.bfloat16),
                (((1,), (1,)), ((), ())),
                preferred_element_type=jnp.float32,
            )
            for q in range(2):
                n = 2 * p + q
                stage[n // 8, pl.ds(n % 8, SLOTS, stride=8), :] = c[
                    q * SLOTS : (q + 1) * SLOTS, :
                ]
        mine = jnp.broadcast_to(self_ref[pl.ds(first, GROUP), :], (GROUP, LANES))
        for h in range(SLOTS):
            out = out_refs[h // per_out]
            column = (h % per_out) * LANES
            tile = jnp.concatenate(
                [stage[0, h * 8 : h * 8 + 8, :], stage[1, h * 8 : h * 8 + 8, :]], axis=0
            )
            out[pl.ds(first, GROUP), column : column + LANES] = tile.astype(jnp.bfloat16)
            hit = jnp.where(mine == lane + h * LANES, 1.0, 0.0)
            out[pl.ds(nodes + first, GROUP), column : column + LANES] = hit.astype(jnp.bfloat16)


def count_blocks(hi, lo, counts, own, n_out, width):
    nodes = own.shape[0]
    vmem = pl.BlockSpec(memory_space=pltpu.VMEM)
    return pl.pallas_call(
        count_kernel,
        out_shape=[jax.ShapeDtypeStruct((2 * nodes, width), jnp.bfloat16)] * n_out,
        in_specs=[vmem] * 4,
        out_specs=[vmem] * n_out,
        scratch_shapes=[pltpu.VMEM((2, SLOTS * 8, LANES), jnp.float32)],
        cost_estimate=pl.CostEstimate(
            flops=9_000_000_000, bytes_accessed=9_000_000, transcendentals=0
        ),
        name="counts",
    )(hi, lo, counts, own)


def shards(items, self_ids, neighbor_ids, visit_counts, w_self, w_neighbor, bias):
    z, yl, x = (lax.axis_index(a) for a in DOM)
    nz, ny, nx = (lax.axis_size(a) for a in DOM)
    core, yh = lax.axis_index("core"), lax.axis_index("yh")
    batch, features = self_ids.shape[0], items.shape[1]
    rows = items.shape[0]
    half = rows // 2

    def places(ids):
        block, r = ids // rows, ids % rows
        dz = (z - block // (ny * nx)) % nz
        dy = (block // nx + yl) % ny
        dx = (x - block) % nx
        part, low = r // half, r % half
        first = (dz * nx + dx) * ny + dy
        second = (dx * nz + dz) * ny + dy
        return jnp.where(part == 0, first, nz * ny * nx + second), low

    partner = shifted(items, "yl", 1)
    halves = [
        jnp.concatenate([items[s : s + half], partner[s : s + half]], axis=0) for s in (0, half)
    ]
    axes = [("x", "z"), ("z", "x")]
    lines = []
    for block, (near, _) in zip(halves, axes):
        others = [shifted(block, near, d) for d in range(1, 4)]
        lines.append(jnp.concatenate([block, *others], axis=0))
    pieces = []
    for line, (_, far) in zip(lines, axes):
        pieces += [line] + [shifted(line, far, d) for d in range(1, 4)]

    hi, lo = places(neighbor_ids)
    own_hi, own_lo = places(self_ids)
    counts_float = visit_counts.astype(jnp.float32)
    nbr = neighbor_ids.shape[1]
    pad = ((0, 0), (0, SLOTS - nbr))
    shift_odd = (jnp.arange(batch, dtype=jnp.int32) % 2 * SLOTS)[:, None]
    pairs = (batch // 2, 2 * SLOTS)
    blocks = count_blocks(
        jnp.pad(hi + shift_odd, pad).reshape(pairs),
        jnp.pad(lo, pad).reshape(pairs),
        jnp.pad(counts_float, pad).reshape(pairs),
        (own_hi * LANES + own_lo)[:, None],
        len(pieces),
        pieces[0].shape[0],
    )
    total = jnp.sum(counts_float, axis=1)

    order = [0, 4, 1, 5, 3, 7, 2, 6]
    sums = sum(
        jnp.dot(blocks[i], pieces[i], preferred_element_type=jnp.float32) for i in order
    )
    own = sums[batch:].astype(jnp.bfloat16)
    pooled = (sums[:batch] / total[:, None]).astype(jnp.bfloat16)

    share = features
    wide = 2 * share
    weights = jnp.concatenate([w_self, w_neighbor], axis=0).reshape(2 * features, 2, 2, share)

    def columns(which):
        return lax.dynamic_index_in_dim(weights, which, 2, False).reshape(2 * features, wide)

    both = jnp.concatenate([own, pooled], axis=1)
    given = jnp.dot(both, columns(1 - core), preferred_element_type=jnp.float32)
    got = shifted(given, "core", 1)
    kept = jnp.dot(both, columns(core), preferred_element_type=jnp.float32)
    chip = kept + got
    there = shifted((chip * SCALE).astype(jnp.float16), "yh", 1)
    pre = chip + there.astype(jnp.float32) * (1.0 / SCALE)
    my_bias = lax.dynamic_index_in_dim(bias.reshape(2, 2, share), core, 1, False).reshape(1, wide)
    hidden = jnp.maximum(pre + my_bias, 0.0)
    squares = jnp.sum(hidden * hidden, axis=1)
    squares = squares + shifted(squares, "core", 1)
    scale = jnp.sqrt(squares / bias.shape[0] + 1e-06)[:, None]
    mine = jnp.where(yh == 0, hidden[:, :share], hidden[:, share:])
    return mine / scale


def solution(mesh):
    torus = Mesh(mesh.devices.reshape(4, 2, 4, 2, 2), ("z", "yl", "x", "yh", "core"))
    feat = ("yh", "core")
    placed = (
        P(DOM, feat),
        P(DOM),
        P(DOM, None),
        P(DOM, None),
        P(feat, None),
        P(feat, None),
        P(),
    )
    return jax.shard_map(
        shards, mesh=torus, in_specs=placed, out_specs=P(DOM, feat), check_vma=False
    )
```

```python
import jax
import jax.numpy as jnp
from jax import lax
from jax.experimental import pallas as pl
from jax.experimental.pallas import tpu as pltpu
from jax.sharding import Mesh
from jax.sharding import PartitionSpec as P


DOM = ("z", "yl", "x")
LANES = 128
SLOTS = 64
GROUP = 16
SCALE = 16.0


def shifted(value, axis, step):
    n = lax.axis_size(axis)
    return lax.ppermute(value, axis, [(i, (i + step) % n) for i in range(n)])


def count_kernel(here_ref, ids_ref, count_ref, self_ref, *rest):
    out_refs, (turned, hi_ref, lo_ref, times_ref, own_hi_ref, own_lo_ref, stage) = rest[:-7], rest[-7:]
    nodes = out_refs[0].shape[0] // 2
    nbr = ids_ref.shape[0]
    here = here_ref[0]
    places = [(o, c) for o in range(len(out_refs)) for c in range(0, out_refs[o].shape[1], LANES)]

    def transposed(top, bottom, blank):
        turned[...] = jnp.full((LANES, LANES), blank, jnp.float32)
        turned[0:nbr, :] = top.astype(jnp.float32)
        turned[SLOTS : SLOTS + nbr, :] = bottom.astype(jnp.float32)
        return turned[...].T

    def column(row):
        return jnp.broadcast_to(row.astype(jnp.float32), (LANES, LANES)).T.astype(jnp.bfloat16)

    hi, lo = located(ids_ref[...], here)
    hi_ref[...] = transposed(hi[:, :LANES], hi[:, LANES:] + SLOTS, -1.0)
    lo_ref[...] = transposed(lo[:, :LANES], lo[:, LANES:], -1.0)
    counts = count_ref[...]
    times_ref[...] = transposed(counts[:, :LANES], counts[:, LANES:], 0.0)
    for part in range(2):
        own_hi, own_lo = located(self_ref[part : part + 1, :], here)
        own_hi_ref[part * LANES : part * LANES + LANES, :] = column(own_hi)
        own_lo_ref[part * LANES : part * LANES + LANES, :] = column(own_lo)

    row = lax.broadcasted_iota(jnp.int32, (GROUP, LANES), 0).astype(jnp.float32)
    rows = [(row + r * GROUP).astype(jnp.bfloat16) for r in range(LANES // GROUP)]
    lane = lax.broadcasted_iota(jnp.int32, (GROUP, LANES), 1).astype(jnp.float32)
    lane = lane.astype(jnp.bfloat16)
    zero = jnp.zeros((GROUP, LANES), jnp.bfloat16)
    one = jnp.ones((GROUP, LANES), jnp.bfloat16)

    @pl.loop(0, LANES // GROUP)
    def _(g):
        first = pl.multiple_of(g * GROUP, GROUP)
        his, los, times = (r[pl.ds(first, GROUP), :] for r in (hi_ref, lo_ref, times_ref))
        for p in range(GROUP):
            h, l, t = (
                jnp.broadcast_to(v[p : p + 1, :], (GROUP, LANES)).astype(jnp.bfloat16)
                for v in (his, los, times)
            )
            c = lax.dot_general(
                jnp.concatenate([jnp.where(h == r, t, zero) for r in rows], axis=0),
                jnp.concatenate([jnp.where(l == r, one, zero) for r in rows], axis=0),
                (((1,), (1,)), ((), ())),
                preferred_element_type=jnp.float32,
            )
            for q in range(2):
                stage[2 * q + p // 8, pl.ds(p % 8, SLOTS, stride=8), :] = c[
                    q * SLOTS : (q + 1) * SLOTS, :
                ]
        for q in range(2):
            base = pl.multiple_of(first + q * LANES, GROUP)
            own_hi = own_hi_ref[pl.ds(base, GROUP), :]
            hit = jnp.where(own_lo_ref[pl.ds(base, GROUP), :] == lane, one, zero)
            for h, (o, col) in enumerate(places):
                tile = jnp.concatenate(
                    [stage[2 * q, h * 8 : h * 8 + 8, :], stage[2 * q + 1, h * 8 : h * 8 + 8, :]],
                    axis=0,
                )
                out_refs[o][pl.ds(base, GROUP), col : col + LANES] = tile.astype(jnp.bfloat16)
                out_refs[o][pl.ds(nodes + base, GROUP), col : col + LANES] = jnp.where(
                    own_hi == jnp.bfloat16(h), hit, zero
                )


def located(ids, here):
    block = ids >> 8
    dz = ((here >> 3) - (block >> 3)) & 3
    dy = ((here >> 2) ^ (block >> 2)) & 1
    dx = (here - block) & 3
    first_half = (ids & 128) == 0
    far = jnp.where(first_half, dz, dx)
    near = jnp.where(first_half, dx, dz)
    turn = far ^ (far >> 1)
    tile = jnp.where(first_half, 0, 32) + turn * 8 + near * 2 + dy
    return tile, ids & 127


def count_blocks(here, ids, counts, own, widths):
    nodes = ids.shape[1]
    vmem = pl.BlockSpec(memory_space=pltpu.VMEM)
    return pl.pallas_call(
        count_kernel,
        out_shape=[jax.ShapeDtypeStruct((2 * nodes, w), jnp.bfloat16) for w in widths],
        in_specs=[pl.BlockSpec(memory_space=pltpu.SMEM)] + [vmem] * 3,
        out_specs=[vmem] * len(widths),
        scratch_shapes=[pltpu.VMEM((LANES, LANES), jnp.float32)] * 4
        + [pltpu.VMEM((nodes, LANES), jnp.bfloat16)] * 2
        + [pltpu.VMEM((4, SLOTS * 8, LANES), jnp.float32)],
        compiler_params=pltpu.CompilerParams(vmem_limit_bytes=16 * 2**20),
        cost_estimate=pl.CostEstimate(
            flops=5_000_000_000, bytes_accessed=9_000_000, transcendentals=0
        ),
        name="counts",
    )(here, ids, counts, own)


def shards(items, self_ids, neighbor_ids, visit_counts, w_self, w_neighbor, bias):
    core, yh = lax.axis_index("core"), lax.axis_index("yh")
    batch, features = self_ids.shape[0], items.shape[1]
    rows = items.shape[0]
    half = rows // 2

    partner = shifted(items, "yl", 1)
    halves = [
        jnp.concatenate([items[s : s + half], partner[s : s + half]], axis=0) for s in (0, half)
    ]
    axes = [("x", "z"), ("z", "x")]
    lines = []
    for block, (near, _) in zip(halves, axes):
        others = [shifted(block, near, d) for d in range(1, 4)]
        lines.append(jnp.concatenate([block, *others], axis=0))
    pieces = []
    for line, (_, far) in zip(lines, axes):
        up, down = shifted(line, far, 1), shifted(line, far, 3)
        middle = line.shape[0] // 2
        pieces += [line, up, down]
        pieces += [shifted(up[:middle], far, 1), shifted(down[middle:], far, 3)]

    ids, counts, _, _ = lax.optimization_barrier((neighbor_ids.T, visit_counts.T, *lines))
    blocks = count_blocks(
        lax.axis_index(DOM).reshape(1),
        ids,
        counts,
        self_ids.reshape(2, LANES),
        [p.shape[0] for p in pieces],
    )
    total = jnp.sum(visit_counts.astype(jnp.float32), axis=1)

    order = [0, 5, 1, 6, 2, 7, 3, 8, 4, 9]
    sums = sum(
        jnp.dot(blocks[i], pieces[i], preferred_element_type=jnp.float32) for i in order
    )
    own = sums[batch:].astype(jnp.bfloat16)
    pooled = (sums[:batch] / total[:, None]).astype(jnp.bfloat16)

    share = features
    wide = 2 * share
    weights = jnp.concatenate([w_self, w_neighbor], axis=0).reshape(2 * features, 2, 2, share)

    def columns(which):
        return lax.dynamic_index_in_dim(weights, which, 2, False).reshape(2 * features, wide)

    both = jnp.concatenate([own, pooled], axis=1)
    given = jnp.dot(both, columns(1 - core), preferred_element_type=jnp.float32)
    got = shifted(given, "core", 1)
    kept = jnp.dot(both, columns(core), preferred_element_type=jnp.float32)
    chip = kept + got
    there = shifted((chip * SCALE).astype(jnp.float16), "yh", 1)
    pre = chip + there.astype(jnp.float32) * (1.0 / SCALE)
    my_bias = lax.dynamic_index_in_dim(bias.reshape(2, 2, share), core, 1, False).reshape(1, wide)
    hidden = jnp.maximum(pre + my_bias, 0.0)
    squares = jnp.sum(hidden * hidden, axis=1)
    squares = squares + shifted(squares, "core", 1)
    scale = jnp.sqrt(squares / bias.shape[0] + 1e-06)[:, None]
    mine = jnp.where(yh == 0, hidden[:, :share], hidden[:, share:])
    return mine / scale


def solution(mesh):
    torus = Mesh(mesh.devices.reshape(4, 2, 4, 2, 2), ("z", "yl", "x", "yh", "core"))
    feat = ("yh", "core")
    placed = (
        P(DOM, feat),
        P(DOM),
        P(DOM, None),
        P(DOM, None),
        P(feat, None),
        P(feat, None),
        P(),
    )
    return jax.shard_map(
        shards, mesh=torus, in_specs=placed, out_specs=P(DOM, feat), check_vma=False
    )
```

```python
import jax
import jax.numpy as jnp
from jax import lax
from jax.experimental import pallas as pl
from jax.experimental.pallas import tpu as pltpu
from jax.sharding import Mesh
from jax.sharding import PartitionSpec as P


DOM = ("z", "yl", "x")
LANES = 128
SLOTS = 64
GROUP = 16
SCALE = 16.0


def shifted(value, axis, step):
    n = lax.axis_size(axis)
    return lax.ppermute(value, axis, [(i, (i + step) % n) for i in range(n)])


def count_kernel(here_ref, ids_ref, count_ref, self_ref, *rest):
    out_refs, (turned, hi_ref, lo_ref, times_ref, own_hi_ref, own_lo_ref, stage) = rest[:-7], rest[-7:]
    nodes = out_refs[0].shape[0] // 2
    nbr = ids_ref.shape[0]
    here = here_ref[0]
    places = [(o, c) for o in range(len(out_refs)) for c in range(0, out_refs[o].shape[1], LANES)]

    def transposed(top, bottom, blank):
        turned[...] = jnp.full((LANES, LANES), blank, jnp.float32)
        turned[0:nbr, :] = top.astype(jnp.float32)
        turned[SLOTS : SLOTS + nbr, :] = bottom.astype(jnp.float32)
        return turned[...].T

    def column(row):
        return jnp.broadcast_to(row.astype(jnp.float32), (LANES, LANES)).T.astype(jnp.bfloat16)

    hi, lo = located(ids_ref[...], here)
    hi_ref[...] = transposed(hi[:, :LANES], hi[:, LANES:] + SLOTS, -1.0)
    lo_ref[...] = transposed(lo[:, :LANES], lo[:, LANES:], -1.0)
    counts = count_ref[...]
    times_ref[...] = transposed(counts[:, :LANES], counts[:, LANES:], 0.0)
    for part in range(2):
        own_hi, own_lo = located(self_ref[part : part + 1, :], here)
        own_hi_ref[part * LANES : part * LANES + LANES, :] = column(own_hi)
        own_lo_ref[part * LANES : part * LANES + LANES, :] = column(own_lo)

    row = lax.broadcasted_iota(jnp.int32, (GROUP, LANES), 0).astype(jnp.float32)
    rows = [(row + r * GROUP).astype(jnp.bfloat16) for r in range(LANES // GROUP)]
    lane = lax.broadcasted_iota(jnp.int32, (GROUP, LANES), 1).astype(jnp.float32)
    lane = lane.astype(jnp.bfloat16)
    zero = jnp.zeros((GROUP, LANES), jnp.bfloat16)
    one = jnp.ones((GROUP, LANES), jnp.bfloat16)

    @pl.loop(0, LANES // GROUP)
    def _(g):
        first = pl.multiple_of(g * GROUP, GROUP)
        his, los, times = (r[pl.ds(first, GROUP), :] for r in (hi_ref, lo_ref, times_ref))
        for p in range(GROUP):
            h, l, t = (
                jnp.broadcast_to(v[p : p + 1, :], (GROUP, LANES)).astype(jnp.bfloat16)
                for v in (his, los, times)
            )
            c = lax.dot_general(
                jnp.concatenate([jnp.where(h == r, t, zero) for r in rows], axis=0),
                jnp.concatenate([jnp.where(l == r, one, zero) for r in rows], axis=0),
                (((1,), (1,)), ((), ())),
                preferred_element_type=jnp.float32,
            )
            for q in range(2):
                stage[2 * q + p // 8, pl.ds(p % 8, SLOTS, stride=8), :] = c[
                    q * SLOTS : (q + 1) * SLOTS, :
                ]
        for q in range(2):
            base = pl.multiple_of(first + q * LANES, GROUP)
            own_hi = own_hi_ref[pl.ds(base, GROUP), :]
            hit = jnp.where(own_lo_ref[pl.ds(base, GROUP), :] == lane, one, zero)
            for h, (o, col) in enumerate(places):
                tile = jnp.concatenate(
                    [stage[2 * q, h * 8 : h * 8 + 8, :], stage[2 * q + 1, h * 8 : h * 8 + 8, :]],
                    axis=0,
                )
                out_refs[o][pl.ds(base, GROUP), col : col + LANES] = tile.astype(jnp.bfloat16)
                out_refs[o][pl.ds(nodes + base, GROUP), col : col + LANES] = jnp.where(
                    own_hi == jnp.bfloat16(h), hit, zero
                )


def located(ids, here):
    block = ids >> 8
    dz = ((here >> 3) - (block >> 3)) & 3
    dy = ((here >> 2) ^ (block >> 2)) & 1
    dx = (here - block) & 3
    first_half = (ids & 128) == 0
    far = jnp.where(first_half, dz, dx)
    near = jnp.where(first_half, dx, dz)
    turn, step = far ^ (far >> 1), near ^ (near >> 1)
    tile = jnp.where(first_half, 0, 32) + turn * 8 + step * 2 + dy
    return tile, ids & 127


def count_blocks(here, ids, counts, own, widths):
    nodes = ids.shape[1]
    vmem = pl.BlockSpec(memory_space=pltpu.VMEM)
    return pl.pallas_call(
        count_kernel,
        out_shape=[jax.ShapeDtypeStruct((2 * nodes, w), jnp.bfloat16) for w in widths],
        in_specs=[pl.BlockSpec(memory_space=pltpu.SMEM)] + [vmem] * 3,
        out_specs=[vmem] * len(widths),
        scratch_shapes=[pltpu.VMEM((LANES, LANES), jnp.float32)] * 4
        + [pltpu.VMEM((nodes, LANES), jnp.bfloat16)] * 2
        + [pltpu.VMEM((4, SLOTS * 8, LANES), jnp.float32)],
        compiler_params=pltpu.CompilerParams(vmem_limit_bytes=16 * 2**20),
        cost_estimate=pl.CostEstimate(
            flops=5_000_000_000, bytes_accessed=9_000_000, transcendentals=0
        ),
        name="counts",
    )(here, ids, counts, own)


def shards(items, self_ids, neighbor_ids, visit_counts, w_self, w_neighbor, bias):
    core, yh = lax.axis_index("core"), lax.axis_index("yh")
    batch, features = self_ids.shape[0], items.shape[1]
    rows = items.shape[0]
    half = rows // 2

    partner = shifted(items, "yl", 1)
    halves = [
        jnp.concatenate([items[s : s + half], partner[s : s + half]], axis=0) for s in (0, half)
    ]
    axes = [("x", "z"), ("z", "x")]
    wide_step = 2 * rows
    lines, ends = [], []
    for block, (near, _) in zip(halves, axes):
        up, down = shifted(block, near, 1), shifted(block, near, 3)
        lines.append(jnp.concatenate([block, up, down], axis=0))
        ends.append(shifted(up, near, 1))
    pieces = []
    for line, end, (_, far) in zip(lines, ends, axes):
        up = shifted(line, far, 1)
        down = shifted(line, far, 3)
        end_up, end_down = shifted(end, far, 1), shifted(end, far, 3)
        rest = jnp.concatenate([down[wide_step:], end_down], axis=0)
        pieces += [line, end, up, end_up, down, end_down]
        pieces += [shifted(up[:wide_step], far, 1), shifted(rest, far, 3)]

    ids, counts, _, _ = lax.optimization_barrier((neighbor_ids.T, visit_counts.T, *ends))
    blocks = count_blocks(
        lax.axis_index(DOM).reshape(1),
        ids,
        counts,
        self_ids.reshape(2, LANES),
        [p.shape[0] for p in pieces],
    )
    total = jnp.sum(visit_counts.astype(jnp.float32), axis=1)

    order = [i + part for i in range(8) for part in (0, 8)]
    sums = sum(
        jnp.dot(blocks[i], pieces[i], preferred_element_type=jnp.float32) for i in order
    )
    own = sums[batch:].astype(jnp.bfloat16)
    pooled = (sums[:batch] / total[:, None]).astype(jnp.bfloat16)

    share = features
    wide = 2 * share
    weights = jnp.concatenate([w_self, w_neighbor], axis=0).reshape(2 * features, 2, 2, share)

    def columns(which):
        return lax.dynamic_index_in_dim(weights, which, 2, False).reshape(2 * features, wide)

    both = jnp.concatenate([own, pooled], axis=1)
    given = jnp.dot(both, columns(1 - core), preferred_element_type=jnp.float32)
    got = shifted(given, "core", 1)
    kept = jnp.dot(both, columns(core), preferred_element_type=jnp.float32)
    chip = kept + got
    there = shifted((chip * SCALE).astype(jnp.float16), "yh", 1)
    pre = chip + there.astype(jnp.float32) * (1.0 / SCALE)
    my_bias = lax.dynamic_index_in_dim(bias.reshape(2, 2, share), core, 1, False).reshape(1, wide)
    hidden = jnp.maximum(pre + my_bias, 0.0)
    squares = jnp.sum(hidden * hidden, axis=1)
    squares = squares + shifted(squares, "core", 1)
    scale = jnp.sqrt(squares / bias.shape[0] + 1e-06)[:, None]
    mine = jnp.where(yh == 0, hidden[:, :share], hidden[:, share:])
    return mine / scale


def solution(mesh):
    torus = Mesh(mesh.devices.reshape(4, 2, 4, 2, 2), ("z", "yl", "x", "yh", "core"))
    feat = ("yh", "core")
    placed = (
        P(DOM, feat),
        P(DOM),
        P(DOM, None),
        P(DOM, None),
        P(feat, None),
        P(feat, None),
        P(),
    )

    return jax.shard_map(
        shards, mesh=torus, in_specs=placed, out_specs=P(DOM, feat), check_vma=False
    )
```

```python
import jax
import jax.numpy as jnp
from jax import lax
from jax.experimental import pallas as pl
from jax.experimental.pallas import tpu as pltpu
from jax.sharding import Mesh
from jax.sharding import PartitionSpec as P


DOM = ("z", "yl", "x")
LANES = 128
SLOTS = 64
TILES = 32
GROUP = 16
SCALE = 16.0


def shifted(value, axis, step):
    n = lax.axis_size(axis)
    return lax.ppermute(value, axis, [(i, (i + step) % n) for i in range(n)])


def count_kernel(here_ref, ids_ref, count_ref, self_ref, *rest):
    out_refs, (turned, hi_ref, lo_ref, times_ref, own_hi_ref, own_lo_ref, stage) = rest[:-7], rest[-7:]
    nodes = out_refs[0].shape[0] // 2
    nbr = ids_ref.shape[0]
    here = here_ref[0]
    places = [(o, c) for o in range(len(out_refs)) for c in range(0, out_refs[o].shape[1], LANES)]

    def transposed(top, bottom, blank):
        turned[...] = jnp.full((LANES, LANES), blank, jnp.float32)
        turned[0:nbr, :] = top.astype(jnp.float32)
        turned[SLOTS : SLOTS + nbr, :] = bottom.astype(jnp.float32)
        return turned[...].T

    def column(row):
        return jnp.broadcast_to(row.astype(jnp.float32), (LANES, LANES)).T.astype(jnp.bfloat16)

    hi, lo = located(ids_ref[...].astype(jnp.int32), here)
    second = jnp.where(hi < 0, hi, hi + TILES)
    hi_ref[...] = transposed(hi[:, :LANES], second[:, LANES:], -1.0)
    lo_ref[...] = transposed(lo[:, :LANES], lo[:, LANES:], -1.0)
    counts = count_ref[...].astype(jnp.int32)
    times_ref[...] = transposed(counts[:, :LANES], counts[:, LANES:], 0.0)
    for part in range(2):
        own_hi, own_lo = located(
            self_ref[part : part + 1, :].astype(jnp.int32), here
        )
        own_hi_ref[part * LANES : part * LANES + LANES, :] = column(own_hi)
        own_lo_ref[part * LANES : part * LANES + LANES, :] = column(own_lo)

    row = lax.broadcasted_iota(jnp.int32, (GROUP, LANES), 0).astype(jnp.float32)
    rows = [(row + r * GROUP).astype(jnp.bfloat16) for r in range(LANES // GROUP)]
    lane = lax.broadcasted_iota(jnp.int32, (GROUP, LANES), 1).astype(jnp.float32)
    lane = lane.astype(jnp.bfloat16)
    zero = jnp.zeros((GROUP, LANES), jnp.bfloat16)
    one = jnp.ones((GROUP, LANES), jnp.bfloat16)

    @pl.loop(0, LANES // GROUP)
    def _(g):
        first = pl.multiple_of(g * GROUP, GROUP)
        his, los, times = (r[pl.ds(first, GROUP), :] for r in (hi_ref, lo_ref, times_ref))
        for p in range(GROUP):
            h, l, t = (
                jnp.broadcast_to(v[p : p + 1, :], (GROUP, LANES)).astype(jnp.bfloat16)
                for v in (his, los, times)
            )
            c = lax.dot_general(
                jnp.concatenate(
                    [jnp.where(h == r, t, zero) for r in rows[: 2 * TILES // GROUP]], axis=0
                ),
                jnp.concatenate([jnp.where(l == r, one, zero) for r in rows], axis=0),
                (((1,), (1,)), ((), ())),
                preferred_element_type=jnp.float32,
            )
            for q in range(2):
                stage[2 * q + p // 8, pl.ds(p % 8, TILES, stride=8), :] = c[
                    q * TILES : (q + 1) * TILES, :
                ]
        for q in range(2):
            base = pl.multiple_of(first + q * LANES, GROUP)
            own_hi = own_hi_ref[pl.ds(base, GROUP), :]
            hit = jnp.where(own_lo_ref[pl.ds(base, GROUP), :] == lane, one, zero)
            for h, (o, col) in enumerate(places):
                tile = jnp.concatenate(
                    [stage[2 * q, h * 8 : h * 8 + 8, :], stage[2 * q + 1, h * 8 : h * 8 + 8, :]],
                    axis=0,
                )
                out_refs[o][pl.ds(base, GROUP), col : col + LANES] = tile.astype(jnp.bfloat16)
                out_refs[o][pl.ds(nodes + base, GROUP), col : col + LANES] = jnp.where(
                    own_hi == jnp.bfloat16(h), hit, zero
                )


def located(ids, here):
    block = ids >> 8
    dz = ((here >> 3) - (block >> 3)) & 3
    dx = (here - block) & 3
    same = (((here ^ block) >> 2) & 1) == 0
    first_half = (ids & 128) == 0
    far = jnp.where(first_half, dz, dx)
    near = jnp.where(first_half, dx, dz)
    tile = jnp.where(first_half, 0, 16) + (far ^ (far >> 1)) * 4 + (near ^ (near >> 1))
    return jnp.where(same, tile, -1), ids & 127


def count_blocks(here, ids, counts, own, widths):
    nodes = ids.shape[1]
    vmem = pl.BlockSpec(memory_space=pltpu.VMEM)
    return pl.pallas_call(
        count_kernel,
        out_shape=[jax.ShapeDtypeStruct((2 * nodes, w), jnp.bfloat16) for w in widths],
        in_specs=[pl.BlockSpec(memory_space=pltpu.SMEM)] + [vmem] * 3,
        out_specs=[vmem] * len(widths),
        scratch_shapes=[pltpu.VMEM((LANES, LANES), jnp.float32)] * 4
        + [pltpu.VMEM((nodes, LANES), jnp.bfloat16)] * 2
        + [pltpu.VMEM((4, TILES * 8, LANES), jnp.float32)],
        compiler_params=pltpu.CompilerParams(vmem_limit_bytes=8 * 2**20),
        cost_estimate=pl.CostEstimate(
            flops=4_000_000_000, bytes_accessed=4_500_000, transcendentals=0
        ),
        name="counts",
    )(here, ids, counts, own)


def shards(items, self_ids, neighbor_ids, visit_counts, w_self, w_neighbor, bias):
    core, yh = lax.axis_index("core"), lax.axis_index("yh")
    batch, share = self_ids.shape[0], items.shape[1]
    nbr = neighbor_ids.shape[1]
    half = items.shape[0] // 2
    here = lax.axis_index(DOM).reshape(1)

    table = jnp.concatenate([neighbor_ids.T, visit_counts.T, self_ids[None, :]], axis=0)
    theirs = shifted(table.astype(jnp.int16), "yl", 1).astype(jnp.int32)

    axes = [("x", "z"), ("z", "x")]
    halves = [items[:half], items[half:]]
    ups = [shifted(block, near, 1) for block, (near, _) in zip(halves, axes)]
    downs = [shifted(block, near, 3) for block, (near, _) in zip(halves, axes)]
    ends = [shifted(up, near, 1) for up, (near, _) in zip(ups, axes)]
    lines = [jnp.concatenate(blocks, axis=0) for blocks in zip(halves, ups, downs, ends)]
    pieces = []
    for line, (_, far) in zip(lines, axes):
        up, down = shifted(line, far, 1), shifted(line, far, 3)
        pieces += [line, up, down, shifted(up, far, 1)]

    widths = [p.shape[0] for p in pieces]
    (mine, *_), (theirs, *_) = (
        lax.optimization_barrier((table, *ups)),
        lax.optimization_barrier((theirs, *lines)),
    )
    rows = []
    for part in (mine, theirs):
        ids, counts, own_ids = part[:nbr], part[nbr : 2 * nbr], part[2 * nbr]
        blocks = count_blocks(here, ids, counts, own_ids.reshape(2, LANES), widths)
        sums = sum(
            jnp.dot(blocks[i], pieces[i], preferred_element_type=jnp.float32)
            for i in (0, 4, 1, 5, 2, 6, 3, 7)
        )
        total = jnp.sum(counts.astype(jnp.float32), axis=0)
        own = sums[batch:].astype(jnp.bfloat16)
        pooled = sums[:batch] / total[:, None]
        high = lax.reduce_precision(pooled, 8, 7)
        rows.append(
            jnp.concatenate(
                [own, high.astype(jnp.bfloat16), (pooled - high).astype(jnp.bfloat16)], axis=1
            )
        )
    both = jnp.concatenate(rows, axis=0)

    wide = 2 * share
    weights = jnp.concatenate([w_self, w_neighbor, w_neighbor], axis=0)
    weights = weights.reshape(3 * share, 2, 2, share)

    def columns(which):
        return lax.dynamic_index_in_dim(weights, which, 2, False).reshape(3 * share, wide)

    given = jnp.dot(both, columns(1 - core), preferred_element_type=jnp.float32)
    got = shifted((given * SCALE).astype(jnp.float16), "core", 1)
    kept = jnp.dot(both, columns(core), preferred_element_type=jnp.float32)
    chip = kept * SCALE + got.astype(jnp.float32)
    sent = chip.astype(jnp.float16)
    from_yh = shifted(sent[:batch], "yh", 1)
    from_yl = shifted(sent[batch:], "yl", 1)
    across = lax.ppermute(sent[batch:], ("yl", "yh"), [(i, i ^ 3) for i in range(4)])
    pre = chip[:batch] + from_yh.astype(jnp.float32)
    pre = pre + from_yl.astype(jnp.float32) + across.astype(jnp.float32)
    my_bias = lax.dynamic_index_in_dim(bias.reshape(2, 2, share), core, 1, False).reshape(1, wide)
    hidden = jnp.maximum(pre * (1.0 / SCALE) + my_bias, 0.0)
    squares = jnp.sum(hidden * hidden, axis=1)
    squares = squares + shifted(squares, "core", 1)
    scale = jnp.sqrt(squares / bias.shape[0] + 1e-06)[:, None]
    out = jnp.where(yh == 0, hidden[:, :share], hidden[:, share:])
    return out / scale


def solution(mesh):
    torus = Mesh(mesh.devices.reshape(4, 2, 4, 2, 2), ("z", "yl", "x", "yh", "core"))
    feat = ("yh", "core")
    placed = (
        P(DOM, feat),
        P(DOM),
        P(DOM, None),
        P(DOM, None),
        P(feat, None),
        P(feat, None),
        P(),
    )
    return jax.shard_map(
        shards, mesh=torus, in_specs=placed, out_specs=P(DOM, feat), check_vma=False
    )
```

```python
import jax
import jax.numpy as jnp
from jax import lax
from jax.experimental import pallas as pl
from jax.experimental.pallas import tpu as pltpu
from jax.sharding import Mesh
from jax.sharding import PartitionSpec as P


DOM = ("z", "yl", "x")
LANES = 128
SLOTS = 64
TILES = 32
EIGHT = 8
GROUP = 16
SCALE = 16.0


def moved(value, axis, target):
    n = lax.axis_size(axis)
    return lax.ppermute(value, axis, [(i, target(i) % n) for i in range(n)])


def count_kernel(here_ref, ids_ref, count_ref, self_ref, *rest):
    out_refs, (turned, code_ref, low_ref, times_ref, own_tile_ref, own_low_ref) = rest[:-6], rest[-6:]
    nodes = out_refs[0].shape[0] // 2
    nbr = ids_ref.shape[0]
    here = here_ref[0]
    places = [(o, c) for o in range(len(out_refs)) for c in range(0, out_refs[o].shape[1], LANES)]

    def column(row):
        return jnp.broadcast_to(row.astype(jnp.float32), (LANES, LANES)).T.astype(jnp.bfloat16)

    node = lax.broadcasted_iota(jnp.int32, (nbr, LANES), 1) & (EIGHT - 1)
    for part in range(nodes // LANES):
        span = pl.ds(part * LANES, LANES)
        tile, low = located(ids_ref[:, span], here)
        code = jnp.where(tile < 0, -1, tile * EIGHT + node)
        for ref, value, blank in (
            (code_ref, code, -1.0),
            (low_ref, low, -1.0),
            (times_ref, count_ref[:, span], 0.0),
        ):
            turned[...] = jnp.full((LANES, LANES), blank, jnp.float32)
            for slot in range(0, LANES, SLOTS):
                turned[slot : slot + nbr, :] = value.astype(jnp.float32)
            ref[span, :] = turned[...].T
        own_tile, own_low = located(self_ref[part : part + 1, :], here)
        own_tile_ref[span, :] = column(own_tile)
        own_low_ref[span, :] = column(own_low)

    row = lax.broadcasted_iota(jnp.int32, (GROUP, LANES), 0).astype(jnp.float32)
    rows = [(row + r * GROUP).astype(jnp.bfloat16) for r in range(TILES * EIGHT // GROUP)]
    lane = lax.broadcasted_iota(jnp.int32, (GROUP, LANES), 1)
    left = lane < SLOTS
    lane = lane.astype(jnp.float32).astype(jnp.bfloat16)
    zero = jnp.zeros((GROUP, LANES), jnp.bfloat16)
    one = jnp.ones((GROUP, LANES), jnp.bfloat16)

    def pair(table, n):
        first, second = (
            jnp.broadcast_to(table[i : i + 1, :], (GROUP, LANES)) for i in (n, n + 1)
        )
        return jnp.where(left, first, second).astype(jnp.bfloat16)

    @pl.loop(0, nodes // GROUP)
    def _(g):
        first = pl.multiple_of(g * GROUP, GROUP)
        span = pl.ds(first, GROUP)
        tables = [r[span, :] for r in (code_ref, low_ref, times_ref)]
        sides = []
        for eight in range(0, GROUP, EIGHT):
            marks, lows = [], []
            for n in range(eight, eight + EIGHT, 2):
                code, low, times = (pair(t, n) for t in tables)
                marks.append(
                    jnp.concatenate([jnp.where(code == r, times, zero) for r in rows], axis=0)
                )
                lows.append(
                    jnp.concatenate(
                        [jnp.where(low == r, one, zero) for r in rows[: LANES // GROUP]], axis=0
                    )
                )
            sides.append(
                lax.dot_general(
                    jnp.concatenate(marks, axis=1),
                    jnp.concatenate(lows, axis=1),
                    (((1,), (1,)), ((), ())),
                    preferred_element_type=jnp.float32,
                )
            )
        own_tile = own_tile_ref[span, :]
        hit = jnp.where(own_low_ref[span, :] == lane, one, zero)
        for t, (o, col) in enumerate(places):
            block = jnp.concatenate([side[t * EIGHT : t * EIGHT + EIGHT, :] for side in sides], axis=0)
            out_refs[o][span, col : col + LANES] = block.astype(jnp.bfloat16)
            out_refs[o][pl.ds(nodes + first, GROUP), col : col + LANES] = jnp.where(
                own_tile == jnp.bfloat16(t), hit, zero
            )


def located(ids, here):
    block = ids >> 8
    dz = ((here >> 3) - (block >> 3)) & 3
    dx = (here - block) & 3
    same = (((here ^ block) >> 2) & 1) == 0
    first_half = (ids & 128) == 0
    far = jnp.where(first_half, dz, dx)
    near = jnp.where(first_half, here ^ block, (here ^ block) >> 3) & 3
    tile = jnp.where(first_half, 0, 16) + (far ^ (far >> 1)) * 4 + (near ^ (near >> 1))
    return jnp.where(same, tile, -1), ids & 127


def count_blocks(here, ids, counts, own, widths):
    nodes = ids.shape[1]
    vmem = pl.BlockSpec(memory_space=pltpu.VMEM)
    return pl.pallas_call(
        count_kernel,
        out_shape=[jax.ShapeDtypeStruct((2 * nodes, w), jnp.bfloat16) for w in widths],
        in_specs=[pl.BlockSpec(memory_space=pltpu.SMEM)] + [vmem] * 3,
        out_specs=[vmem] * len(widths),
        scratch_shapes=[pltpu.VMEM((LANES, LANES), jnp.float32)]
        + [pltpu.VMEM((nodes, LANES), jnp.float32)] * 3
        + [pltpu.VMEM((nodes, LANES), jnp.bfloat16)] * 2,
        compiler_params=pltpu.CompilerParams(vmem_limit_bytes=16 * 2**20),
        cost_estimate=pl.CostEstimate(
            flops=4_000_000_000, bytes_accessed=9_000_000, transcendentals=0
        ),
        name="counts",
    )(here, ids, counts, own)


def shards(items, self_ids, neighbor_ids, visit_counts, w_self, w_neighbor, bias):
    core, yh = lax.axis_index("core"), lax.axis_index("yh")
    batch, share = self_ids.shape[0], items.shape[1]
    nbr = neighbor_ids.shape[1]
    half = items.shape[0] // 2
    here = lax.axis_index(DOM).reshape(1)

    table = jnp.concatenate([neighbor_ids.T, visit_counts.T, self_ids[None, :]], axis=0)
    theirs = moved(table.astype(jnp.int16), "yl", lambda i: i ^ 1).astype(jnp.int32)
    table = jnp.concatenate([table, theirs], axis=1)
    ids, counts, own_ids = table[:nbr], table[nbr : 2 * nbr], table[2 * nbr]

    axes = [("x", "z"), ("z", "x")]
    halves = [items[:half], items[half:]]
    lines = []
    for block, (near, _) in zip(halves, axes):
        pair = jnp.concatenate([block, moved(block, near, lambda i: i ^ 1)], axis=0)
        lines.append(jnp.concatenate([pair, moved(pair, near, lambda i: i ^ 3)], axis=0))
    pieces = []
    for line, (_, far) in zip(lines, axes):
        up, down = moved(line, far, lambda i: i + 1), moved(line, far, lambda i: i + 3)
        pieces += [line, up, down, moved(up, far, lambda i: i + 1)]

    blocks = count_blocks(
        here, ids, counts, own_ids.reshape(-1, LANES), [p.shape[0] for p in pieces]
    )
    sums = sum(
        jnp.dot(blocks[i], pieces[i], preferred_element_type=jnp.float32)
        for i in (0, 4, 1, 5, 2, 6, 3, 7)
    )
    total = jnp.sum(counts.astype(jnp.float32), axis=0)
    own = sums[2 * batch :].astype(jnp.bfloat16)
    pooled = sums[: 2 * batch] / total[:, None]
    high = lax.reduce_precision(pooled, 8, 7)
    both = jnp.concatenate(
        [own, high.astype(jnp.bfloat16), (pooled - high).astype(jnp.bfloat16)], axis=1
    )

    wide = 2 * share
    weights = jnp.concatenate([w_self, w_neighbor, w_neighbor], axis=0)
    weights = weights.reshape(3 * share, 2, 2, share)

    def columns(which):
        return lax.dynamic_index_in_dim(weights, which, 2, False).reshape(3 * share, wide)

    given = jnp.dot(both, columns(1 - core), preferred_element_type=jnp.float32)
    got = moved((given * SCALE).astype(jnp.float16), "core", lambda i: i ^ 1)
    kept = jnp.dot(both, columns(core), preferred_element_type=jnp.float32)
    kept = lax.optimization_barrier(kept)
    chip = kept * SCALE + got.astype(jnp.float32)
    sent = chip.astype(jnp.float16)
    from_yh = moved(sent[:batch], "yh", lambda i: i ^ 1)
    from_yl = moved(sent[batch:], "yl", lambda i: i ^ 1)
    across = lax.ppermute(sent[batch:], ("yl", "yh"), [(i, i ^ 3) for i in range(4)])
    pre = chip[:batch] + from_yh.astype(jnp.float32)
    pre = pre + from_yl.astype(jnp.float32) + across.astype(jnp.float32)
    my_bias = lax.dynamic_index_in_dim(bias.reshape(2, 2, share), core, 1, False).reshape(1, wide)
    hidden = jnp.maximum(pre * (1.0 / SCALE) + my_bias, 0.0)
    squares = jnp.sum(hidden * hidden, axis=1)
    squares = squares + moved(squares, "core", lambda i: i ^ 1)
    scale = jnp.sqrt(squares / bias.shape[0] + 1e-06)[:, None]
    out = jnp.where(yh == 0, hidden[:, :share], hidden[:, share:])
    return out / scale


def solution(mesh):
    torus = Mesh(mesh.devices.reshape(4, 2, 4, 2, 2), ("z", "yl", "x", "yh", "core"))
    feat = ("yh", "core")
    placed = (
        P(DOM, feat),
        P(DOM),
        P(DOM, None),
        P(DOM, None),
        P(feat, None),
        P(feat, None),
        P(),
    )

    return jax.shard_map(
        shards, mesh=torus, in_specs=placed, out_specs=P(DOM, feat), check_vma=False
    )
```

```python
import functools

import jax
import jax.numpy as jnp
from jax import lax
from jax.experimental import pallas as pl
from jax.experimental.pallas import tpu as pltpu
from jax.sharding import Mesh
from jax.sharding import PartitionSpec as P


DOM = ("z", "yl", "x")
LANES = 128
SLOTS = 64
TILES = 32
EIGHT = 8
GROUP = 16
SCALE = 16.0


def moved(value, axis, target):
    n = lax.axis_size(axis)
    return lax.ppermute(value, axis, [(i, target(i) % n) for i in range(n)])


def count_kernel(group, n_given, here_ref, ids_ref, count_ref, self_ref, *rest):
    rest = rest[n_given:]
    out_refs, (turned, code_ref, low_ref, times_ref, own_tile_ref, own_low_ref) = rest[:-6], rest[-6:]
    nbr, nodes = ids_ref.shape
    counts_row, own_row = group * nodes, (2 + group) * nodes
    here = here_ref[0]
    places = [(o, c) for o in range(len(out_refs)) for c in range(0, out_refs[o].shape[1], LANES)]

    def column(row):
        return jnp.broadcast_to(row.astype(jnp.float32), (LANES, LANES)).T.astype(jnp.bfloat16)

    node = lax.broadcasted_iota(jnp.int32, (nbr, LANES), 1) & (EIGHT - 1)
    for part in range(nodes // LANES):
        span = pl.ds(part * LANES, LANES)
        tile, low = located(ids_ref[:, span], here)
        code = jnp.where(tile < 0, -1, tile * EIGHT + node)
        for ref, value, blank in (
            (code_ref, code, -1.0),
            (low_ref, low, -1.0),
            (times_ref, count_ref[:, span], 0.0),
        ):
            turned[...] = jnp.full((LANES, LANES), blank, jnp.float32)
            for slot in range(0, LANES, SLOTS):
                turned[slot : slot + nbr, :] = value.astype(jnp.float32)
            ref[span, :] = turned[...].T
        own_tile, own_low = located(self_ref[part : part + 1, :], here)
        own_tile_ref[span, :] = column(own_tile)
        own_low_ref[span, :] = column(own_low)

    row = lax.broadcasted_iota(jnp.int32, (GROUP, LANES), 0).astype(jnp.float32)
    rows = [(row + r * GROUP).astype(jnp.bfloat16) for r in range(TILES * EIGHT // GROUP)]
    lane = lax.broadcasted_iota(jnp.int32, (GROUP, LANES), 1)
    left = lane < SLOTS
    lane = lane.astype(jnp.float32).astype(jnp.bfloat16)
    zero = jnp.zeros((GROUP, LANES), jnp.bfloat16)
    one = jnp.ones((GROUP, LANES), jnp.bfloat16)

    def pair(table, n):
        first, second = (
            jnp.broadcast_to(table[i : i + 1, :], (GROUP, LANES)) for i in (n, n + 1)
        )
        return jnp.where(left, first, second).astype(jnp.bfloat16)

    @pl.loop(0, nodes // GROUP, unroll=2)
    def _(g):
        first = pl.multiple_of(g * GROUP, GROUP)
        span = pl.ds(first, GROUP)
        tables = [r[span, :] for r in (code_ref, low_ref, times_ref)]
        sides = []
        for eight in range(0, GROUP, EIGHT):
            marks, lows = [], []
            for n in range(eight, eight + EIGHT, 2):
                code, low, times = (pair(t, n) for t in tables)
                marks.append(
                    jnp.concatenate([jnp.where(code == r, times, zero) for r in rows], axis=0)
                )
                lows.append(
                    jnp.concatenate(
                        [jnp.where(low == r, one, zero) for r in rows[: LANES // GROUP]], axis=0
                    )
                )
            sides.append(
                lax.dot_general(
                    jnp.concatenate(marks, axis=1),
                    jnp.concatenate(lows, axis=1),
                    (((1,), (1,)), ((), ())),
                    preferred_element_type=jnp.float32,
                )
            )
        own_tile = own_tile_ref[span, :]
        hit = jnp.where(own_low_ref[span, :] == lane, one, zero)
        for t, (o, col) in enumerate(places):
            block = jnp.concatenate([side[t * EIGHT : t * EIGHT + EIGHT, :] for side in sides], axis=0)
            out_refs[o][pl.ds(counts_row + first, GROUP), col : col + LANES] = block.astype(jnp.bfloat16)
            out_refs[o][pl.ds(own_row + first, GROUP), col : col + LANES] = jnp.where(
                own_tile == jnp.bfloat16(t), hit, zero
            )


def located(ids, here):
    block = ids >> 8
    dz = ((here >> 3) - (block >> 3)) & 3
    dx = (here - block) & 3
    same = (((here ^ block) >> 2) & 1) == 0
    first_half = (ids & 128) == 0
    far = jnp.where(first_half, dz, dx)
    near = jnp.where(first_half, here ^ block, (here ^ block) >> 3) & 3
    tile = jnp.where(first_half, 0, 16) + (far ^ (far >> 1)) * 4 + (near ^ (near >> 1))
    return jnp.where(same, tile, -1), ids & 127


def count_blocks(group, given, here, table, nbr, widths):
    nodes = table.shape[1]
    vmem = pl.BlockSpec(memory_space=pltpu.VMEM)
    return pl.pallas_call(
        functools.partial(count_kernel, group, len(given)),
        out_shape=[jax.ShapeDtypeStruct((4 * nodes, w), jnp.bfloat16) for w in widths],
        in_specs=[pl.BlockSpec(memory_space=pltpu.SMEM)] + [vmem] * (3 + len(given)),
        out_specs=[vmem] * len(widths),
        input_output_aliases={4 + i: i for i in range(len(given))},
        scratch_shapes=[pltpu.VMEM((LANES, LANES), jnp.float32)]
        + [pltpu.VMEM((nodes, LANES), jnp.float32)] * 3
        + [pltpu.VMEM((nodes, LANES), jnp.bfloat16)] * 2,
        compiler_params=pltpu.CompilerParams(vmem_limit_bytes=16 * 2**20),
        cost_estimate=pl.CostEstimate(
            flops=2_000_000_000, bytes_accessed=4_500_000, transcendentals=0
        ),
        name="counts",
    )(
        here,
        table[:nbr],
        table[nbr : 2 * nbr],
        table[2 * nbr].reshape(nodes // LANES, LANES),
        *given,
    )


def shards(items, self_ids, neighbor_ids, visit_counts, w_self, w_neighbor, bias):
    core, yh = lax.axis_index("core"), lax.axis_index("yh")
    batch, share = self_ids.shape[0], items.shape[1]
    nbr = neighbor_ids.shape[1]
    half = items.shape[0] // 2
    here = lax.axis_index(DOM).reshape(1)

    table = jnp.concatenate([neighbor_ids.T, visit_counts.T, self_ids[None, :]], axis=0)
    theirs = moved(table.astype(jnp.int16), "yl", lambda i: i ^ 1).astype(jnp.int32)

    axes = [("x", "z"), ("z", "x")]
    halves = [items[:half], items[half:]]
    lines = []
    for block, (near, _) in zip(halves, axes):
        pair = jnp.concatenate([block, moved(block, near, lambda i: i ^ 1)], axis=0)
        rest = moved(pair, near, lambda i: i ^ 3)
        lines.append(jnp.concatenate([pair, rest], axis=0))
    pieces = []
    for line, (_, far) in zip(lines, axes):
        up, down = moved(line, far, lambda i: i + 1), moved(line, far, lambda i: i + 3)
        pieces += [line, up, down, moved(up, far, lambda i: i + 1)]

    widths = [p.shape[0] for p in pieces]
    blocks = count_blocks(0, [], here, table, nbr, widths)
    blocks = count_blocks(1, blocks, here, theirs, nbr, widths)
    sums = sum(
        jnp.dot(blocks[i], pieces[i], preferred_element_type=jnp.float32)
        for i in (0, 4, 1, 5, 2, 6, 3, 7)
    )
    total = jnp.concatenate(
        [jnp.sum(t[nbr : 2 * nbr].astype(jnp.float32), axis=0) for t in (table, theirs)]
    )
    own = sums[2 * batch :].astype(jnp.bfloat16)
    pooled = sums[: 2 * batch] / total[:, None]
    high = lax.reduce_precision(pooled, 8, 7)
    both = jnp.concatenate(
        [own, high.astype(jnp.bfloat16), (pooled - high).astype(jnp.bfloat16)], axis=1
    )

    wide = 2 * share
    weights = jnp.concatenate([w_self, w_neighbor, w_neighbor], axis=0)

    def columns(which):
        firsts = [which * share, wide + which * share]
        cut = [lax.dynamic_slice_in_dim(weights, first, share, 1) for first in firsts]
        return jnp.concatenate(cut, axis=1)

    given = jnp.dot(both, columns(1 - core), preferred_element_type=jnp.float32)
    got = moved((given * SCALE).astype(jnp.float16), "core", lambda i: i ^ 1)
    kept = jnp.dot(both, columns(core), preferred_element_type=jnp.float32)
    kept = lax.optimization_barrier(kept)
    chip = kept * SCALE + got.astype(jnp.float32)
    sent = chip.astype(jnp.float16)
    from_yh = moved(sent[:batch], "yh", lambda i: i ^ 1)
    from_yl = moved(sent[batch:], "yl", lambda i: i ^ 1)
    across = lax.ppermute(sent[batch:], ("yl", "yh"), [(i, i ^ 3) for i in range(4)])
    pre = chip[:batch] + from_yh.astype(jnp.float32)
    pre = pre + from_yl.astype(jnp.float32) + across.astype(jnp.float32)
    my_bias = lax.dynamic_index_in_dim(bias.reshape(2, 2, share), core, 1, False).reshape(1, wide)
    hidden = jnp.maximum(pre * (1.0 / SCALE) + my_bias, 0.0)
    squares = jnp.sum(hidden * hidden, axis=1)
    squares = squares + moved(squares, "core", lambda i: i ^ 1)
    scale = jnp.sqrt(squares / bias.shape[0] + 1e-06)[:, None]
    out = jnp.where(yh == 0, hidden[:, :share], hidden[:, share:])
    return out / scale


def solution(mesh):
    torus = Mesh(mesh.devices.reshape(4, 2, 4, 2, 2), ("z", "yl", "x", "yh", "core"))
    feat = ("yh", "core")
    placed = (
        P(DOM, feat),
        P(DOM),
        P(DOM, None),
        P(DOM, None),
        P(feat, None),
        P(feat, None),
        P(),
    )

    return jax.shard_map(
        shards, mesh=torus, in_specs=placed, out_specs=P(DOM, feat), check_vma=False
    )
```

```python
import functools

import jax
import jax.numpy as jnp
from jax import lax
from jax.experimental import pallas as pl
from jax.experimental.pallas import tpu as pltpu
from jax.sharding import Mesh
from jax.sharding import PartitionSpec as P


DOM = ("z", "yl", "x")
LANES = 128
SLOTS = 64
TILES = 16
WIDE = 2 * LANES
EIGHT = 8
GROUP = 16
SCALE = 16.0


def moved(value, axis, target):
    n = lax.axis_size(axis)
    return lax.ppermute(value, axis, [(i, target(i) % n) for i in range(n)])


def count_kernel(group, n_given, here_ref, ids_ref, count_ref, self_ref, *rest):
    rest = rest[n_given:]
    out_refs, (turned, code_ref, low_ref, times_ref, own_tile_ref, own_low_ref) = rest[:-6], rest[-6:]
    nbr, nodes = ids_ref.shape
    counts_row, own_row = group * nodes, (2 + group) * nodes
    here = here_ref[0]
    places = [(o, c) for o in range(len(out_refs)) for c in range(0, out_refs[o].shape[1], WIDE)]

    def column(row):
        return jnp.broadcast_to(row.astype(jnp.float32), (LANES, LANES)).T.astype(jnp.bfloat16)

    def widened(value):
        return jnp.concatenate([value] * (WIDE // LANES), axis=1)

    node = lax.broadcasted_iota(jnp.int32, (nbr, LANES), 1) & (EIGHT - 1)
    for part in range(nodes // LANES):
        span = pl.ds(part * LANES, LANES)
        tile, low = located(ids_ref[:, span], here)
        code = jnp.where(tile < 0, -1, tile * EIGHT + node)
        for ref, value, blank in (
            (code_ref, code, -1.0),
            (low_ref, low, -1.0),
            (times_ref, count_ref[:, span], 0.0),
        ):
            turned[...] = jnp.full((LANES, LANES), blank, jnp.float32)
            for slot in range(0, LANES, SLOTS):
                turned[slot : slot + nbr, :] = value.astype(jnp.float32)
            ref[span, :] = turned[...].T
        own_tile, own_low = located(self_ref[part : part + 1, :], here)
        own_tile_ref[span, :] = column(own_tile)
        own_low_ref[span, :] = column(own_low)

    row = lax.broadcasted_iota(jnp.int32, (GROUP, LANES), 0).astype(jnp.float32)
    rows = [(row + r * GROUP).astype(jnp.bfloat16) for r in range(WIDE // GROUP)]
    left = lax.broadcasted_iota(jnp.int32, (GROUP, LANES), 1) < SLOTS
    lane = lax.broadcasted_iota(jnp.int32, (GROUP, WIDE), 1)
    lane = lane.astype(jnp.float32).astype(jnp.bfloat16)
    zero = jnp.zeros((GROUP, LANES), jnp.bfloat16)
    one = jnp.ones((GROUP, LANES), jnp.bfloat16)

    def pair(table, n):
        first, second = (
            jnp.broadcast_to(table[i : i + 1, :], (GROUP, LANES)) for i in (n, n + 1)
        )
        return jnp.where(left, first, second).astype(jnp.bfloat16)

    @pl.loop(0, nodes // GROUP, unroll=2)
    def _(g):
        first = pl.multiple_of(g * GROUP, GROUP)
        span = pl.ds(first, GROUP)
        tables = [r[span, :] for r in (code_ref, low_ref, times_ref)]
        sides = []
        for eight in range(0, GROUP, EIGHT):
            marks, lows = [], []
            for n in range(eight, eight + EIGHT, 2):
                code, low, times = (pair(t, n) for t in tables)
                marks.append(
                    jnp.concatenate(
                        [jnp.where(code == r, times, zero) for r in rows[: TILES * EIGHT // GROUP]],
                        axis=0,
                    )
                )
                lows.append(
                    jnp.concatenate([jnp.where(low == r, one, zero) for r in rows], axis=0)
                )
            sides.append(
                lax.dot_general(
                    jnp.concatenate(marks, axis=1),
                    jnp.concatenate(lows, axis=1),
                    (((1,), (1,)), ((), ())),
                    preferred_element_type=jnp.float32,
                )
            )
        own_tile = widened(own_tile_ref[span, :])
        hit = jnp.where(widened(own_low_ref[span, :]) == lane, widened(one), widened(zero))
        for t, (o, col) in enumerate(places):
            block = jnp.concatenate([side[t * EIGHT : t * EIGHT + EIGHT, :] for side in sides], axis=0)
            out_refs[o][pl.ds(counts_row + first, GROUP), col : col + WIDE] = block.astype(jnp.bfloat16)
            out_refs[o][pl.ds(own_row + first, GROUP), col : col + WIDE] = jnp.where(
                own_tile == jnp.bfloat16(t), hit, widened(zero)
            )


def located(ids, here):
    block = ids >> 8
    dz = ((here >> 3) - (block >> 3)) & 3
    dx = (here - block) & 3
    same = (((here ^ block) >> 2) & 1) == 0
    first_half = (ids & 128) == 0
    far = jnp.where(first_half, dz, dx)
    near = jnp.where(first_half, here ^ block, (here ^ block) >> 3) & 3
    tile = jnp.where(first_half, 0, 16) + (far ^ (far >> 1)) * 4 + (near ^ (near >> 1))
    return jnp.where(same, tile >> 1, -1), ((tile & 1) << 7) + (ids & 127)


def count_blocks(group, given, here, table, nbr, widths):
    nodes = table.shape[1]
    vmem = pl.BlockSpec(memory_space=pltpu.VMEM)
    return pl.pallas_call(
        functools.partial(count_kernel, group, len(given)),
        out_shape=[jax.ShapeDtypeStruct((4 * nodes, w), jnp.bfloat16) for w in widths],
        in_specs=[pl.BlockSpec(memory_space=pltpu.SMEM)] + [vmem] * (3 + len(given)),
        out_specs=[vmem] * len(widths),
        input_output_aliases={4 + i: i for i in range(len(given))},
        scratch_shapes=[pltpu.VMEM((LANES, LANES), jnp.float32)]
        + [pltpu.VMEM((nodes, LANES), jnp.float32)] * 3
        + [pltpu.VMEM((nodes, LANES), jnp.bfloat16)] * 2,
        compiler_params=pltpu.CompilerParams(vmem_limit_bytes=16 * 2**20),
        cost_estimate=pl.CostEstimate(
            flops=2_000_000_000, bytes_accessed=4_500_000, transcendentals=0
        ),
        name="counts",
    )(
        here,
        table[:nbr],
        table[nbr : 2 * nbr],
        table[2 * nbr].reshape(nodes // LANES, LANES),
        *given,
    )


def project_kernel(which_ref, sums_ref, total_ref, self_ref, nbr_ref, out_ref):
    nodes, share = sums_ref.shape[0] // 2, sums_ref.shape[1]
    total = jnp.concatenate([total_ref[...]] * (share // LANES), axis=1)
    own = sums_ref[nodes:, :].astype(jnp.bfloat16)
    pooled = sums_ref[:nodes, :] / total
    high = pooled.astype(jnp.bfloat16)
    low = (pooled - high.astype(jnp.float32)).astype(jnp.bfloat16)
    for part in range(2):
        first = pl.multiple_of(part * 2 * share + which_ref[0] * share, share)
        columns = pl.ds(first, share)
        w_self, w_nbr = self_ref[:, columns], nbr_ref[:, columns]
        out = jnp.dot(own, w_self, preferred_element_type=jnp.float32)
        out += jnp.dot(high, w_nbr, preferred_element_type=jnp.float32)
        out += jnp.dot(low, w_nbr, preferred_element_type=jnp.float32)
        out_ref[:, part * share : (part + 1) * share] = out * SCALE


def projected(which, sums, total, w_self, w_neighbor):
    nodes, share = sums.shape[0] // 2, sums.shape[1]
    vmem = pl.BlockSpec(memory_space=pltpu.VMEM)
    return pl.pallas_call(
        project_kernel,
        out_shape=jax.ShapeDtypeStruct((nodes, 2 * share), jnp.float32),
        in_specs=[pl.BlockSpec(memory_space=pltpu.SMEM)] + [vmem] * 4,
        out_specs=vmem,
        compiler_params=pltpu.CompilerParams(vmem_limit_bytes=12 * 2**20),
        cost_estimate=pl.CostEstimate(
            flops=400_000_000, bytes_accessed=4_000_000, transcendentals=0
        ),
        name="project",
    )(which.reshape(1), sums, total, w_self, w_neighbor)


def shards(items, self_ids, neighbor_ids, visit_counts, w_self, w_neighbor, bias):
    core, yh = lax.axis_index("core"), lax.axis_index("yh")
    batch, share = self_ids.shape[0], items.shape[1]
    nbr = neighbor_ids.shape[1]
    half = items.shape[0] // 2
    here = lax.axis_index(DOM).reshape(1)

    table = jnp.concatenate([neighbor_ids.T, visit_counts.T, self_ids[None, :]], axis=0)
    theirs = moved(table.astype(jnp.int16), "yl", lambda i: i ^ 1).astype(jnp.int32)

    axes = [("x", "z"), ("z", "x")]
    halves = [items[:half], items[half:]]
    lines = []
    for block, (near, _) in zip(halves, axes):
        pair = jnp.concatenate([block, moved(block, near, lambda i: i ^ 1)], axis=0)
        rest = moved(pair, near, lambda i: i ^ 3)
        lines.append(jnp.concatenate([pair, rest], axis=0))
    pieces = []
    for line, (_, far) in zip(lines, axes):
        up, down = moved(line, far, lambda i: i + 1), moved(line, far, lambda i: i + 3)
        pieces += [line, up, down, moved(up, far, lambda i: i + 1)]

    widths = [p.shape[0] for p in pieces]
    blocks = count_blocks(0, [], here, table, nbr, widths)
    blocks = count_blocks(1, blocks, here, theirs, nbr, widths)
    sums = sum(
        jnp.dot(blocks[i], pieces[i], preferred_element_type=jnp.float32)
        for i in (0, 4, 1, 5, 2, 6, 3, 7)
    )
    wide = 2 * share
    total = jnp.concatenate(
        [jnp.sum(t[nbr : 2 * nbr].astype(jnp.float32), axis=0) for t in (table, theirs)]
    )
    total = jnp.broadcast_to(total[:, None], (2 * batch, LANES))
    given = projected(1 - core, sums, total, w_self, w_neighbor)
    got = moved(given.astype(jnp.float16), "core", lambda i: i ^ 1)
    kept = projected(core, sums, total, w_self, w_neighbor)
    chip = kept + got.astype(jnp.float32)
    sent = chip.astype(jnp.float16)
    from_yh = moved(sent[:batch], "yh", lambda i: i ^ 1)
    from_yl = moved(sent[batch:], "yl", lambda i: i ^ 1)
    across = lax.ppermute(sent[batch:], ("yl", "yh"), [(i, i ^ 3) for i in range(4)])
    pre = chip[:batch] + from_yh.astype(jnp.float32)
    pre = pre + from_yl.astype(jnp.float32) + across.astype(jnp.float32)
    my_bias = lax.dynamic_index_in_dim(bias.reshape(2, 2, share), core, 1, False).reshape(1, wide)
    hidden = jnp.maximum(pre * (1.0 / SCALE) + my_bias, 0.0)
    squares = jnp.sum(hidden * hidden, axis=1)
    squares = squares + moved(squares, "core", lambda i: i ^ 1)
    scale = jnp.sqrt(squares / bias.shape[0] + 1e-06)[:, None]
    out = jnp.where(yh == 0, hidden[:, :share], hidden[:, share:])
    return out / scale


def solution(mesh):
    torus = Mesh(mesh.devices.reshape(4, 2, 4, 2, 2), ("z", "yl", "x", "yh", "core"))
    feat = ("yh", "core")
    placed = (
        P(DOM, feat),
        P(DOM),
        P(DOM, None),
        P(DOM, None),
        P(feat, None),
        P(feat, None),
        P(),
    )

    return jax.shard_map(
        shards, mesh=torus, in_specs=placed, out_specs=P(DOM, feat), check_vma=False
    )
```

```python
import functools

import jax
import jax.numpy as jnp
from jax import lax
from jax.experimental import pallas as pl
from jax.experimental.pallas import tpu as pltpu
from jax.sharding import Mesh
from jax.sharding import PartitionSpec as P


DOM = ("z", "yl", "x")
LANES = 128
SLOTS = 64
TILES = 32
EIGHT = 8
GROUP = 16
SCALE = 16.0


def moved(value, axis, target):
    n = lax.axis_size(axis)
    return lax.ppermute(value, axis, [(i, target(i) % n) for i in range(n)])


def count_kernel(group, n_given, here_ref, ids_ref, count_ref, self_ref, *rest):
    rest = rest[n_given:]
    out_refs, (turned, code_ref, low_ref, times_ref, own_tile_ref, own_low_ref) = rest[:-6], rest[-6:]
    nbr, nodes = ids_ref.shape
    counts_row, own_row = group * nodes, (2 + group) * nodes
    here = here_ref[0]
    places = [(o, c) for o in range(len(out_refs)) for c in range(0, out_refs[o].shape[1], LANES)]

    def column(row):
        return jnp.broadcast_to(row.astype(jnp.float32), (LANES, LANES)).T.astype(jnp.bfloat16)

    node = lax.broadcasted_iota(jnp.int32, (nbr, LANES), 1) & (EIGHT - 1)
    for part in range(nodes // LANES):
        span = pl.ds(part * LANES, LANES)
        tile, low = located(ids_ref[:, span], here)
        code = jnp.where(tile < 0, -1, tile * EIGHT + node)
        for ref, value, blank in (
            (code_ref, code, -1.0),
            (low_ref, low, -1.0),
            (times_ref, count_ref[:, span], 0.0),
        ):
            turned[...] = jnp.full((LANES, LANES), blank, jnp.float32)
            for slot in range(0, LANES, SLOTS):
                turned[slot : slot + nbr, :] = value.astype(jnp.float32)
            ref[span, :] = turned[...].T
        own_tile, own_low = located(self_ref[part : part + 1, :], here)
        own_tile_ref[span, :] = column(own_tile)
        own_low_ref[span, :] = column(own_low)

    row = lax.broadcasted_iota(jnp.int32, (GROUP, LANES), 0).astype(jnp.float32)
    rows = [(row + r * GROUP).astype(jnp.bfloat16) for r in range(TILES * EIGHT // GROUP)]
    lane = lax.broadcasted_iota(jnp.int32, (GROUP, LANES), 1)
    left = lane < SLOTS
    lane = lane.astype(jnp.float32).astype(jnp.bfloat16)
    zero = jnp.zeros((GROUP, LANES), jnp.bfloat16)
    one = jnp.ones((GROUP, LANES), jnp.bfloat16)

    def pair(table, n):
        first, second = (
            jnp.broadcast_to(table[i : i + 1, :], (GROUP, LANES)) for i in (n, n + 1)
        )
        return jnp.where(left, first, second).astype(jnp.bfloat16)

    @pl.loop(0, nodes // GROUP, unroll=2)
    def _(g):
        first = pl.multiple_of(g * GROUP, GROUP)
        span = pl.ds(first, GROUP)
        tables = [r[span, :] for r in (code_ref, low_ref, times_ref)]
        sides = []
        for eight in range(0, GROUP, EIGHT):
            marks, lows = [], []
            for n in range(eight, eight + EIGHT, 2):
                code, low, times = (pair(t, n) for t in tables)
                marks.append(
                    jnp.concatenate([jnp.where(code == r, times, zero) for r in rows], axis=0)
                )
                lows.append(
                    jnp.concatenate(
                        [jnp.where(low == r, one, zero) for r in rows[: LANES // GROUP]], axis=0
                    )
                )
            sides.append(
                lax.dot_general(
                    jnp.concatenate(marks, axis=1),
                    jnp.concatenate(lows, axis=1),
                    (((1,), (1,)), ((), ())),
                    preferred_element_type=jnp.float32,
                )
            )
        own_tile = own_tile_ref[span, :]
        hit = jnp.where(own_low_ref[span, :] == lane, one, zero)
        for t, (o, col) in enumerate(places):
            block = jnp.concatenate([side[t * EIGHT : t * EIGHT + EIGHT, :] for side in sides], axis=0)
            out_refs[o][pl.ds(counts_row + first, GROUP), col : col + LANES] = block.astype(jnp.bfloat16)
            out_refs[o][pl.ds(own_row + first, GROUP), col : col + LANES] = jnp.where(
                own_tile == jnp.bfloat16(t), hit, zero
            )


def located(ids, here):
    apart = here ^ (ids >> 8)
    same = ((apart >> 2) & 1) == 0
    dx, dz = apart & 3, (apart >> 3) & 3
    first_half = (ids & 128) == 0
    far = jnp.where(first_half, dz, dx)
    near = jnp.where(first_half, dx, dz)
    tile = jnp.where(first_half, 0, 16) + (far ^ (far >> 1)) * 4 + (near ^ (near >> 1))
    return jnp.where(same, tile, -1), ids & 127


def count_blocks(group, given, here, table, nbr, widths):
    nodes = table.shape[1]
    vmem = pl.BlockSpec(memory_space=pltpu.VMEM)
    return pl.pallas_call(
        functools.partial(count_kernel, group, len(given)),
        out_shape=[jax.ShapeDtypeStruct((4 * nodes, w), jnp.bfloat16) for w in widths],
        in_specs=[pl.BlockSpec(memory_space=pltpu.SMEM)] + [vmem] * (3 + len(given)),
        out_specs=[vmem] * len(widths),
        input_output_aliases={4 + i: i for i in range(len(given))},
        scratch_shapes=[pltpu.VMEM((LANES, LANES), jnp.float32)]
        + [pltpu.VMEM((nodes, LANES), jnp.float32)] * 3
        + [pltpu.VMEM((nodes, LANES), jnp.bfloat16)] * 2,
        compiler_params=pltpu.CompilerParams(vmem_limit_bytes=16 * 2**20),
        cost_estimate=pl.CostEstimate(
            flops=2_000_000_000, bytes_accessed=4_500_000, transcendentals=0
        ),
        name="counts",
    )(
        here,
        table[:nbr],
        table[nbr : 2 * nbr],
        table[2 * nbr].reshape(nodes // LANES, LANES),
        *given,
    )


def project_kernel(which_ref, sums_ref, total_ref, self_ref, nbr_ref, out_ref):
    nodes, share = sums_ref.shape[0] // 2, sums_ref.shape[1]
    total = jnp.concatenate([total_ref[...]] * (share // LANES), axis=1)
    own = sums_ref[nodes:, :].astype(jnp.bfloat16)
    pooled = sums_ref[:nodes, :] / total
    high = pooled.astype(jnp.bfloat16)
    low = (pooled - high.astype(jnp.float32)).astype(jnp.bfloat16)
    for part in range(2):
        first = pl.multiple_of(part * 2 * share + which_ref[0] * share, share)
        columns = pl.ds(first, share)
        w_self, w_nbr = self_ref[:, columns], nbr_ref[:, columns]
        out = jnp.dot(own, w_self, preferred_element_type=jnp.float32)
        out += jnp.dot(high, w_nbr, preferred_element_type=jnp.float32)
        out += jnp.dot(low, w_nbr, preferred_element_type=jnp.float32)
        out_ref[:, part * share : (part + 1) * share] = out * SCALE


def projected(which, sums, total, w_self, w_neighbor):
    nodes, share = sums.shape[0] // 2, sums.shape[1]
    vmem = pl.BlockSpec(memory_space=pltpu.VMEM)
    return pl.pallas_call(
        project_kernel,
        out_shape=jax.ShapeDtypeStruct((nodes, 2 * share), jnp.float32),
        in_specs=[pl.BlockSpec(memory_space=pltpu.SMEM)] + [vmem] * 4,
        out_specs=vmem,
        compiler_params=pltpu.CompilerParams(vmem_limit_bytes=12 * 2**20),
        cost_estimate=pl.CostEstimate(
            flops=400_000_000, bytes_accessed=4_000_000, transcendentals=0
        ),
        name="project",
    )(which.reshape(1), sums, total, w_self, w_neighbor)


def shards(items, self_ids, neighbor_ids, visit_counts, w_self, w_neighbor, bias):
    core, yh = lax.axis_index("core"), lax.axis_index("yh")
    batch, share = self_ids.shape[0], items.shape[1]
    nbr = neighbor_ids.shape[1]
    half = items.shape[0] // 2
    here = lax.axis_index(DOM).reshape(1)

    table = jnp.concatenate([neighbor_ids.T, visit_counts.T, self_ids[None, :]], axis=0)
    theirs = moved(table.astype(jnp.int16), "yl", lambda i: i ^ 1).astype(jnp.int32)

    axes = [("x", "z"), ("z", "x")]
    halves = [items[:half], items[half:]]
    lines = []
    for block, (near, _) in zip(halves, axes):
        pair = jnp.concatenate([block, moved(block, near, lambda i: i ^ 1)], axis=0)
        rest = moved(pair, near, lambda i: i ^ 3)
        lines.append(jnp.concatenate([pair, rest], axis=0))
    pieces = []
    for line, (_, far) in zip(lines, axes):
        low, high = moved(line, far, lambda i: i ^ 1), moved(line, far, lambda i: i ^ 3)
        pieces += [line, low, high, moved(high, far, lambda i: i ^ 1)]

    widths = [p.shape[0] for p in pieces]
    blocks = count_blocks(0, [], here, table, nbr, widths)
    blocks = count_blocks(1, blocks, here, theirs, nbr, widths)
    sums = sum(
        jnp.dot(blocks[i], pieces[i], preferred_element_type=jnp.float32)
        for i in (0, 4, 1, 5, 2, 6, 3, 7)
    )
    total = jnp.concatenate(
        [jnp.sum(t[nbr : 2 * nbr].astype(jnp.float32), axis=0) for t in (table, theirs)]
    )
    total = jnp.broadcast_to(total[:, None], (2 * batch, LANES))
    given = projected(1 - core, sums, total, w_self, w_neighbor)
    got = moved(given.astype(jnp.float16), "core", lambda i: i ^ 1)
    kept = projected(core, sums, total, w_self, w_neighbor)
    chip = kept + got.astype(jnp.float32)
    first, second = chip[:, :share], chip[:, share:]
    here_part = jnp.where(yh == 0, first, second)
    there_part = jnp.where(yh == 0, second, first).astype(jnp.float16)
    from_yh = moved(there_part[:batch], "yh", lambda i: i ^ 1)
    from_yl = moved(here_part[batch:].astype(jnp.float16), "yl", lambda i: i ^ 1)
    across = lax.ppermute(there_part[batch:], ("yl", "yh"), [(i, i ^ 3) for i in range(4)])
    pre = here_part[:batch] + from_yh.astype(jnp.float32)
    pre = pre + from_yl.astype(jnp.float32) + across.astype(jnp.float32)
    my_bias = lax.dynamic_slice_in_dim(bias, (2 * yh + core) * share, share, 0)
    hidden = jnp.maximum(pre * (1.0 / SCALE) + my_bias[None, :], 0.0)
    squares = jnp.sum(hidden * hidden, axis=1)
    squares = squares + moved(squares, "core", lambda i: i ^ 1)
    squares = squares + moved(squares, "yh", lambda i: i ^ 1)
    scale = jnp.sqrt(squares / bias.shape[0] + 1e-06)[:, None]
    return hidden / scale


def solution(mesh):
    torus = Mesh(mesh.devices.reshape(4, 2, 4, 2, 2), ("z", "yl", "x", "yh", "core"))
    feat = ("yh", "core")
    placed = (
        P(DOM, feat),
        P(DOM),
        P(DOM, None),
        P(DOM, None),
        P(feat, None),
        P(feat, None),
        P(),
    )

    return jax.shard_map(
        shards, mesh=torus, in_specs=placed, out_specs=P(DOM, feat), check_vma=False
    )
```

```python
import functools

import jax
import jax.numpy as jnp
from jax import lax
from jax.experimental import pallas as pl
from jax.experimental.pallas import tpu as pltpu
from jax.sharding import Mesh
from jax.sharding import PartitionSpec as P


DOM = ("z", "yl", "x")
LANES = 128
SLOTS = 64
TILES = 32
EIGHT = 8
GROUP = 16
SCALE = 16.0


def moved(value, axis, target):
    n = lax.axis_size(axis)
    return lax.ppermute(value, axis, [(i, target(i) % n) for i in range(n)])


def count_kernel(group, n_given, here_ref, ids_ref, count_ref, self_ref, *rest):
    rest = rest[n_given:]
    out_refs, (turned, code_ref, low_ref, times_ref, own_tile_ref, own_low_ref) = rest[:-6], rest[-6:]
    nbr, nodes = ids_ref.shape
    counts_row, own_row = group * nodes, (2 + group) * nodes
    here = here_ref[0]
    places = [(o, c) for o in range(len(out_refs)) for c in range(0, out_refs[o].shape[1], LANES)]

    def column(row):
        return jnp.broadcast_to(row.astype(jnp.float32), (LANES, LANES)).T.astype(jnp.bfloat16)

    node = lax.broadcasted_iota(jnp.int32, (nbr, LANES), 1) & (EIGHT - 1)
    for part in range(nodes // LANES):
        span = pl.ds(part * LANES, LANES)
        tile, low = located(ids_ref[:, span], here)
        code = jnp.where(tile < 0, -1, tile * EIGHT + node)
        for ref, value, blank in (
            (code_ref, code, -1.0),
            (low_ref, low, -1.0),
            (times_ref, count_ref[:, span], 0.0),
        ):
            turned[...] = jnp.full((LANES, LANES), blank, jnp.float32)
            for slot in range(0, LANES, SLOTS):
                turned[slot : slot + nbr, :] = value.astype(jnp.float32)
            ref[span, :] = turned[...].T
        own_tile, own_low = located(self_ref[part : part + 1, :], here)
        own_tile_ref[span, :] = column(own_tile)
        own_low_ref[span, :] = column(own_low)

    row = lax.broadcasted_iota(jnp.int32, (GROUP, LANES), 0).astype(jnp.float32)
    rows = [(row + r * GROUP).astype(jnp.bfloat16) for r in range(TILES * EIGHT // GROUP)]
    lane = lax.broadcasted_iota(jnp.int32, (GROUP, LANES), 1)
    left = lane < SLOTS
    lane = lane.astype(jnp.float32).astype(jnp.bfloat16)
    zero = jnp.zeros((GROUP, LANES), jnp.bfloat16)
    one = jnp.ones((GROUP, LANES), jnp.bfloat16)

    def pair(table, n):
        first, second = (
            jnp.broadcast_to(table[i : i + 1, :], (GROUP, LANES)) for i in (n, n + 1)
        )
        return jnp.where(left, first, second).astype(jnp.bfloat16)

    @pl.loop(0, nodes // GROUP, unroll=2)
    def _(g):
        first = pl.multiple_of(g * GROUP, GROUP)
        span = pl.ds(first, GROUP)
        tables = [r[span, :] for r in (code_ref, low_ref, times_ref)]
        sides = []
        for eight in range(0, GROUP, EIGHT):
            marks, lows = [], []
            for n in range(eight, eight + EIGHT, 2):
                code, low, times = (pair(t, n) for t in tables)
                marks.append(
                    jnp.concatenate([jnp.where(code == r, times, zero) for r in rows], axis=0)
                )
                lows.append(
                    jnp.concatenate(
                        [jnp.where(low == r, one, zero) for r in rows[: LANES // GROUP]], axis=0
                    )
                )
            sides.append(
                lax.dot_general(
                    jnp.concatenate(marks, axis=1),
                    jnp.concatenate(lows, axis=1),
                    (((1,), (1,)), ((), ())),
                    preferred_element_type=jnp.float32,
                )
            )
        own_tile = own_tile_ref[span, :]
        hit = jnp.where(own_low_ref[span, :] == lane, one, zero)
        for t, (o, col) in enumerate(places):
            block = jnp.concatenate([side[t * EIGHT : t * EIGHT + EIGHT, :] for side in sides], axis=0)
            out_refs[o][pl.ds(counts_row + first, GROUP), col : col + LANES] = block.astype(jnp.bfloat16)
            out_refs[o][pl.ds(own_row + first, GROUP), col : col + LANES] = jnp.where(
                own_tile == jnp.bfloat16(t), hit, zero
            )


def located(ids, here):
    apart = here ^ (ids >> 8)
    same = ((apart >> 2) & 1) == 0
    dx, dz = apart & 3, (apart >> 3) & 3
    first_half = (ids & 128) == 0
    far = jnp.where(first_half, dz, dx)
    near = jnp.where(first_half, dx, dz)
    tile = jnp.where(first_half, 0, 16) + (far ^ (far >> 1)) * 4 + (near ^ (near >> 1))
    return jnp.where(same, tile, -1), ids & 127


def count_blocks(group, given, here, table, nbr, widths):
    nodes = table.shape[1]
    vmem = pl.BlockSpec(memory_space=pltpu.VMEM)
    return pl.pallas_call(
        functools.partial(count_kernel, group, len(given)),
        out_shape=[jax.ShapeDtypeStruct((4 * nodes, w), jnp.bfloat16) for w in widths],
        in_specs=[pl.BlockSpec(memory_space=pltpu.SMEM)] + [vmem] * (3 + len(given)),
        out_specs=[vmem] * len(widths),
        input_output_aliases={4 + i: i for i in range(len(given))},
        scratch_shapes=[pltpu.VMEM((LANES, LANES), jnp.float32)]
        + [pltpu.VMEM((nodes, LANES), jnp.float32)] * 3
        + [pltpu.VMEM((nodes, LANES), jnp.bfloat16)] * 2,
        compiler_params=pltpu.CompilerParams(vmem_limit_bytes=16 * 2**20),
        cost_estimate=pl.CostEstimate(
            flops=2_000_000_000, bytes_accessed=4_500_000, transcendentals=0
        ),
        name="counts",
    )(
        here,
        table[:nbr],
        table[nbr : 2 * nbr],
        table[2 * nbr].reshape(nodes // LANES, LANES),
        *given,
    )


def project_kernel(which_ref, sums_ref, total_ref, self_ref, nbr_ref, out_ref):
    nodes, share = sums_ref.shape[0] // 2, sums_ref.shape[1]
    total = jnp.concatenate([total_ref[...]] * (share // LANES), axis=1)
    own = sums_ref[nodes:, :].astype(jnp.bfloat16)
    pooled = sums_ref[:nodes, :] / total
    high = pooled.astype(jnp.bfloat16)
    low = (pooled - high.astype(jnp.float32)).astype(jnp.bfloat16)
    for part in range(2):
        first = pl.multiple_of(part * 2 * share + which_ref[0] * share, share)
        columns = pl.ds(first, share)
        w_self, w_nbr = self_ref[:, columns], nbr_ref[:, columns]
        out = jnp.dot(own, w_self, preferred_element_type=jnp.float32)
        out += jnp.dot(high, w_nbr, preferred_element_type=jnp.float32)
        out += jnp.dot(low, w_nbr, preferred_element_type=jnp.float32)
        out_ref[:, part * share : (part + 1) * share] = out * SCALE


def projected(which, sums, total, w_self, w_neighbor):
    nodes, share = sums.shape[0] // 2, sums.shape[1]
    vmem = pl.BlockSpec(memory_space=pltpu.VMEM)
    return pl.pallas_call(
        project_kernel,
        out_shape=jax.ShapeDtypeStruct((nodes, 2 * share), jnp.float32),
        in_specs=[pl.BlockSpec(memory_space=pltpu.SMEM)] + [vmem] * 4,
        out_specs=vmem,
        compiler_params=pltpu.CompilerParams(vmem_limit_bytes=12 * 2**20),
        cost_estimate=pl.CostEstimate(
            flops=400_000_000, bytes_accessed=4_000_000, transcendentals=0
        ),
        name="project",
    )(which.reshape(1), sums, total, w_self, w_neighbor)


def shards(items, self_ids, neighbor_ids, visit_counts, w_self, w_neighbor, bias):
    core, yh = lax.axis_index("core"), lax.axis_index("yh")
    batch, share = self_ids.shape[0], items.shape[1]
    nbr = neighbor_ids.shape[1]
    half = items.shape[0] // 2
    here = lax.axis_index(DOM).reshape(1)

    table = jnp.concatenate([neighbor_ids.T, visit_counts.T, self_ids[None, :]], axis=0)
    sent = lax.optimization_barrier(table).astype(jnp.int16)
    theirs = moved(sent, "yl", lambda i: i ^ 1).astype(jnp.int32)

    axes = [("x", "z"), ("z", "x")]
    halves = [items[:half], items[half:]]
    lines = []
    for block, (near, _) in zip(halves, axes):
        pair = jnp.concatenate([block, moved(block, near, lambda i: i ^ 1)], axis=0)
        rest = moved(pair, near, lambda i: i ^ 3)
        lines.append(jnp.concatenate([pair, rest], axis=0))
    pieces = []
    for line, (_, far) in zip(lines, axes):
        low = moved(line, far, lambda i: i ^ 1)
        high = moved(line, far, lambda i: i ^ 3)
        middle = line.shape[0] // 2
        last = [
            moved(high[:middle], far, lambda i: i ^ 1), moved(low[middle:], far, lambda i: i ^ 3)
        ]
        pieces += [line, low, high, jnp.concatenate(last, axis=0)]

    widths = [p.shape[0] for p in pieces]
    blocks = count_blocks(0, [], here, table, nbr, widths)
    blocks = count_blocks(1, blocks, here, theirs, nbr, widths)
    sums = sum(
        jnp.dot(blocks[i], pieces[i], preferred_element_type=jnp.float32)
        for i in (0, 4, 1, 5, 2, 6, 3, 7)
    )
    total = jnp.concatenate(
        [jnp.sum(t[nbr : 2 * nbr].astype(jnp.float32), axis=0) for t in (table, theirs)]
    )
    total = jnp.broadcast_to(total[:, None], (2 * batch, LANES))
    given = projected(1 - core, sums, total, w_self, w_neighbor)
    got = moved(given.astype(jnp.float16), "core", lambda i: i ^ 1)
    kept = projected(core, sums, total, w_self, w_neighbor)
    chip = kept + got.astype(jnp.float32)
    first, second = chip[:, :share], chip[:, share:]
    here_part = jnp.where(yh == 0, first, second)
    there_part = jnp.where(yh == 0, second, first).astype(jnp.float16)
    from_yh = moved(there_part[:batch], "yh", lambda i: i ^ 1)
    from_yl = moved(here_part[batch:].astype(jnp.float16), "yl", lambda i: i ^ 1)
    across = lax.ppermute(there_part[batch:], ("yl", "yh"), [(i, i ^ 3) for i in range(4)])
    pre = here_part[:batch] + from_yh.astype(jnp.float32)
    pre = pre + from_yl.astype(jnp.float32) + across.astype(jnp.float32)
    my_bias = lax.dynamic_slice_in_dim(bias, (2 * yh + core) * share, share, 0)
    hidden = jnp.maximum(pre * (1.0 / SCALE) + my_bias[None, :], 0.0)
    squares = jnp.sum(hidden * hidden, axis=1)
    squares = squares + moved(squares, "core", lambda i: i ^ 1)
    squares = squares + moved(squares, "yh", lambda i: i ^ 1)
    scale = jnp.sqrt(squares / bias.shape[0] + 1e-06)[:, None]
    return hidden / scale


def solution(mesh):
    torus = Mesh(mesh.devices.reshape(4, 2, 4, 2, 2), ("z", "yl", "x", "yh", "core"))
    feat = ("yh", "core")
    placed = (
        P(DOM, feat),
        P(DOM),
        P(DOM, None),
        P(DOM, None),
        P(feat, None),
        P(feat, None),
        P(),
    )

    return jax.shard_map(
        shards, mesh=torus, in_specs=placed, out_specs=P(DOM, feat), check_vma=False
    )
```

```python
import functools

import jax
import jax.numpy as jnp
from jax import lax
from jax.experimental import pallas as pl
from jax.experimental.pallas import tpu as pltpu
from jax.sharding import Mesh
from jax.sharding import PartitionSpec as P


DOM = ("z", "yl", "x")
LANES = 128
SLOTS = 64
TILES = 32
EIGHT = 8
GROUP = 16
SCALE = 16.0


def moved(value, axis, target):
    n = lax.axis_size(axis)
    return lax.ppermute(value, axis, [(i, target(i) % n) for i in range(n)])


def count_kernel(group, n_given, here_ref, ids_ref, count_ref, self_ref, *rest):
    rest = rest[n_given:]
    out_refs, (turned, code_ref, low_ref, times_ref, own_tile_ref, own_low_ref) = rest[:-6], rest[-6:]
    nbr, nodes = ids_ref.shape
    counts_row, own_row = group * nodes, (2 + group) * nodes
    here = here_ref[0] >> 1
    places = [(o, c) for o in range(len(out_refs)) for c in range(0, out_refs[o].shape[1], LANES)]

    def column(row):
        return jnp.broadcast_to(row.astype(jnp.float32), (LANES, LANES)).T.astype(jnp.bfloat16)

    node = lax.broadcasted_iota(jnp.int32, (nbr, LANES), 1) & (EIGHT - 1)
    for part in range(nodes // LANES):
        span = pl.ds(part * LANES, LANES)
        tile, low = located(ids_ref[:, span], here)
        code = jnp.where(tile < 0, -1, tile * EIGHT + node)
        for ref, value, blank in (
            (code_ref, code, -1.0),
            (low_ref, low, -1.0),
            (times_ref, count_ref[:, span], 0.0),
        ):
            turned[...] = jnp.full((LANES, LANES), blank, jnp.float32)
            for slot in range(0, LANES, SLOTS):
                turned[slot : slot + nbr, :] = value.astype(jnp.float32)
            ref[span, :] = turned[...].T
        own_tile, own_low = located(self_ref[part : part + 1, :], here)
        own_tile_ref[span, :] = column(own_tile)
        own_low_ref[span, :] = column(own_low)

    row = lax.broadcasted_iota(jnp.int32, (GROUP, LANES), 0).astype(jnp.float32)
    rows = [(row + r * GROUP).astype(jnp.bfloat16) for r in range(TILES * EIGHT // GROUP)]
    lane = lax.broadcasted_iota(jnp.int32, (GROUP, LANES), 1)
    left = lane < SLOTS
    lane = lane.astype(jnp.float32).astype(jnp.bfloat16)
    zero = jnp.zeros((GROUP, LANES), jnp.bfloat16)
    one = jnp.ones((GROUP, LANES), jnp.bfloat16)

    def pair(table, n):
        first, second = (
            jnp.broadcast_to(table[i : i + 1, :], (GROUP, LANES)) for i in (n, n + 1)
        )
        return jnp.where(left, first, second).astype(jnp.bfloat16)

    @pl.loop(0, nodes // GROUP, unroll=2)
    def _(g):
        first = pl.multiple_of(g * GROUP, GROUP)
        span = pl.ds(first, GROUP)
        tables = [r[span, :] for r in (code_ref, low_ref, times_ref)]
        sides = []
        for eight in range(0, GROUP, EIGHT):
            marks, lows = [], []
            for n in range(eight, eight + EIGHT, 2):
                code, low, times = (pair(t, n) for t in tables)
                marks.append(
                    jnp.concatenate([jnp.where(code == r, times, zero) for r in rows], axis=0)
                )
                lows.append(
                    jnp.concatenate(
                        [jnp.where(low == r, one, zero) for r in rows[: LANES // GROUP]], axis=0
                    )
                )
            sides.append(
                lax.dot_general(
                    jnp.concatenate(marks, axis=1),
                    jnp.concatenate(lows, axis=1),
                    (((1,), (1,)), ((), ())),
                    preferred_element_type=jnp.float32,
                )
            )
        own_tile = own_tile_ref[span, :]
        hit = jnp.where(own_low_ref[span, :] == lane, one, zero)
        for t, (o, col) in enumerate(places):
            block = jnp.concatenate([side[t * EIGHT : t * EIGHT + EIGHT, :] for side in sides], axis=0)
            out_refs[o][pl.ds(counts_row + first, GROUP), col : col + LANES] = block.astype(jnp.bfloat16)
            out_refs[o][pl.ds(own_row + first, GROUP), col : col + LANES] = jnp.where(
                own_tile == jnp.bfloat16(t), hit, zero
            )


def located(ids, here):
    apart = here ^ (ids >> 8)
    same = ((apart >> 2) & 1) == 0
    dx, dz = apart & 3, (apart >> 3) & 3
    first_half = (ids & 128) == 0
    far = jnp.where(first_half, dz, dx)
    near = jnp.where(first_half, dx, dz)
    tile = jnp.where(first_half, 0, 16) + (far ^ (far >> 1)) * 4 + (near ^ (near >> 1))
    return jnp.where(same, tile, -1), ids & 127


def count_blocks(group, given, here, table, nbr, widths):
    nodes = table.shape[1]
    vmem = pl.BlockSpec(memory_space=pltpu.VMEM)
    return pl.pallas_call(
        functools.partial(count_kernel, group, len(given)),
        out_shape=[jax.ShapeDtypeStruct((4 * nodes, w), jnp.bfloat16) for w in widths],
        in_specs=[pl.BlockSpec(memory_space=pltpu.SMEM)] + [vmem] * (3 + len(given)),
        out_specs=[vmem] * len(widths),
        input_output_aliases={4 + i: i for i in range(len(given))},
        scratch_shapes=[pltpu.VMEM((LANES, LANES), jnp.float32)]
        + [pltpu.VMEM((nodes, LANES), jnp.float32)] * 3
        + [pltpu.VMEM((nodes, LANES), jnp.bfloat16)] * 2,
        compiler_params=pltpu.CompilerParams(vmem_limit_bytes=16 * 2**20),
        cost_estimate=pl.CostEstimate(
            flops=2_000_000_000, bytes_accessed=4_500_000, transcendentals=0
        ),
        name="counts",
    )(
        here,
        table[:nbr],
        table[nbr : 2 * nbr],
        table[2 * nbr].reshape(nodes // LANES, LANES),
        *given,
    )


def project_kernel(flip, here_ref, sums_ref, total_ref, self_ref, nbr_ref, out_ref):
    nodes, share = sums_ref.shape[0] // 2, sums_ref.shape[1]
    total = jnp.concatenate([total_ref[...]] * (share // LANES), axis=1)
    own = sums_ref[nodes:, :].astype(jnp.bfloat16)
    pooled = sums_ref[:nodes, :] / total
    high = pooled.astype(jnp.bfloat16)
    low = (pooled - high.astype(jnp.float32)).astype(jnp.bfloat16)
    which = (here_ref[0] & 1) ^ flip
    for part in range(2):
        first = pl.multiple_of(part * 2 * share + which * share, share)
        columns = pl.ds(first, share)
        w_self, w_nbr = self_ref[:, columns], nbr_ref[:, columns]
        out = jnp.dot(own, w_self, preferred_element_type=jnp.float32)
        out += jnp.dot(high, w_nbr, preferred_element_type=jnp.float32)
        out += jnp.dot(low, w_nbr, preferred_element_type=jnp.float32)
        out_ref[:, part * share : (part + 1) * share] = out * SCALE


def projected(flip, here, sums, total, w_self, w_neighbor):
    nodes, share = sums.shape[0] // 2, sums.shape[1]
    vmem = pl.BlockSpec(memory_space=pltpu.VMEM)
    return pl.pallas_call(
        functools.partial(project_kernel, flip),
        out_shape=jax.ShapeDtypeStruct((nodes, 2 * share), jnp.float32),
        in_specs=[pl.BlockSpec(memory_space=pltpu.SMEM)] + [vmem] * 4,
        out_specs=vmem,
        compiler_params=pltpu.CompilerParams(vmem_limit_bytes=12 * 2**20),
        cost_estimate=pl.CostEstimate(
            flops=400_000_000, bytes_accessed=4_000_000, transcendentals=0
        ),
        name="project",
    )(here, sums, total, w_self, w_neighbor)


def shards(items, self_ids, neighbor_ids, visit_counts, w_self, w_neighbor, bias):
    core, yh = lax.axis_index("core"), lax.axis_index("yh")
    batch, share = self_ids.shape[0], items.shape[1]
    nbr = neighbor_ids.shape[1]
    half = items.shape[0] // 2
    here = lax.axis_index((*DOM, "core")).reshape(1)

    axes = [("x", "z"), ("z", "x")]
    halves = [items[:half], items[half:]]
    lines = []
    for block, (near, _) in zip(halves, axes):
        pair = jnp.concatenate([block, moved(block, near, lambda i: i ^ 1)], axis=0)
        rest = moved(pair, near, lambda i: i ^ 3)
        lines.append(jnp.concatenate([pair, rest], axis=0))
    pieces = []
    for line, (_, far) in zip(lines, axes):
        low = moved(line, far, lambda i: i ^ 1)
        high = moved(line, far, lambda i: i ^ 3)
        pieces += [line, low, high, moved(high, far, lambda i: i ^ 1)]

    table = (neighbor_ids.T, visit_counts.T, self_ids)
    kept_back, _ = lax.optimization_barrier((table, lines))
    sent = lax.optimization_barrier(
        jnp.concatenate([kept_back[0], kept_back[1], kept_back[2][None, :]], axis=0)
    )
    theirs = moved(sent.astype(jnp.int16), "yl", lambda i: i ^ 1).astype(jnp.int32)
    table = jnp.concatenate([table[0], table[1], table[2][None, :]], axis=0)
    widths = [p.shape[0] for p in pieces]
    blocks = count_blocks(0, [], here, table, nbr, widths)
    blocks = count_blocks(1, blocks, here, theirs, nbr, widths)
    sums = sum(
        jnp.dot(blocks[i], pieces[i], preferred_element_type=jnp.float32)
        for i in (0, 4, 1, 5, 2, 6, 3, 7)
    )
    total = jnp.concatenate(
        [jnp.sum(t[nbr : 2 * nbr].astype(jnp.float32), axis=0) for t in (table, theirs)]
    )
    total = jnp.broadcast_to(total[:, None], (2 * batch, LANES))
    given = projected(1, here, sums, total, w_self, w_neighbor)
    got = moved(given.astype(jnp.float16), "core", lambda i: i ^ 1)
    kept = projected(0, here, sums, total, w_self, w_neighbor)
    chip = kept + got.astype(jnp.float32)
    first, second = chip[:, :share], chip[:, share:]
    here_part = jnp.where(yh == 0, first, second)
    there_part = jnp.where(yh == 0, second, first).astype(jnp.float16)
    from_yh = moved(there_part[:batch], "yh", lambda i: i ^ 1)
    from_yl = moved(here_part[batch:].astype(jnp.float16), "yl", lambda i: i ^ 1)
    across = lax.ppermute(there_part[batch:], ("yl", "yh"), [(i, i ^ 3) for i in range(4)])
    pre = here_part[:batch] + from_yh.astype(jnp.float32)
    pre = pre + from_yl.astype(jnp.float32) + across.astype(jnp.float32)
    my_bias = lax.dynamic_slice_in_dim(bias, (2 * yh + core) * share, share, 0)
    hidden = jnp.maximum(pre * (1.0 / SCALE) + my_bias[None, :], 0.0)
    squares = jnp.sum(hidden * hidden, axis=1)
    squares = squares + moved(squares, "core", lambda i: i ^ 1)
    squares = squares + moved(squares, "yh", lambda i: i ^ 1)
    scale = jnp.sqrt(squares / bias.shape[0] + 1e-06)[:, None]
    return hidden / scale


def solution(mesh):
    torus = Mesh(mesh.devices.reshape(4, 2, 4, 2, 2), ("z", "yl", "x", "yh", "core"))
    feat = ("yh", "core")
    placed = (
        P(DOM, feat),
        P(DOM),
        P(DOM, None),
        P(DOM, None),
        P(feat, None),
        P(feat, None),
        P(),
    )

    return jax.shard_map(
        shards, mesh=torus, in_specs=placed, out_specs=P(DOM, feat), check_vma=False
    )
```

```python
import functools

import jax
import jax.numpy as jnp
from jax import lax
from jax.experimental import pallas as pl
from jax.experimental.pallas import tpu as pltpu
from jax.sharding import Mesh
from jax.sharding import PartitionSpec as P


DOM = ("z", "yl", "x")
LANES = 128
SLOTS = 64
TILES = 32
EIGHT = 8
GROUP = 16
SCALE = 16.0


def moved(value, axis, target):
    n = lax.axis_size(axis)
    return lax.ppermute(value, axis, [(i, target(i) % n) for i in range(n)])


def count_kernel(group, n_given, here_ref, ids_ref, count_ref, self_ref, *rest):
    rest = rest[n_given:]
    out_refs, (turned, code_ref, low_ref, times_ref, own_tile_ref, own_low_ref) = rest[:-6], rest[-6:]
    nbr, nodes = ids_ref.shape
    counts_row, own_row = group * nodes, (2 + group) * nodes
    here = here_ref[0] >> 1
    places = [(o, c) for o in range(len(out_refs)) for c in range(0, out_refs[o].shape[1], LANES)]

    def column(row):
        return jnp.broadcast_to(row.astype(jnp.float32), (LANES, LANES)).T.astype(jnp.bfloat16)

    node = lax.broadcasted_iota(jnp.int32, (nbr, LANES), 1) & (EIGHT - 1)
    for part in range(nodes // LANES):
        span = pl.ds(part * LANES, LANES)
        tile, low = located(ids_ref[:, span], here)
        code = jnp.where(tile < 0, -1, tile * EIGHT + node)
        for ref, value, blank in (
            (code_ref, code, -1.0),
            (low_ref, low, -1.0),
            (times_ref, count_ref[:, span], 0.0),
        ):
            turned[...] = jnp.full((LANES, LANES), blank, jnp.float32)
            for slot in range(0, LANES, SLOTS):
                turned[slot : slot + nbr, :] = value.astype(jnp.float32)
            ref[span, :] = turned[...].T
        own_tile, own_low = located(self_ref[part : part + 1, :], here)
        own_tile_ref[span, :] = column(own_tile)
        own_low_ref[span, :] = column(own_low)

    row = lax.broadcasted_iota(jnp.int32, (GROUP, LANES), 0).astype(jnp.float32)
    rows = [(row + r * GROUP).astype(jnp.bfloat16) for r in range(TILES * EIGHT // GROUP)]
    lane = lax.broadcasted_iota(jnp.int32, (GROUP, LANES), 1)
    left = lane < SLOTS
    lane = lane.astype(jnp.float32).astype(jnp.bfloat16)
    zero = jnp.zeros((GROUP, LANES), jnp.bfloat16)
    one = jnp.ones((GROUP, LANES), jnp.bfloat16)

    def pair(table, n):
        first, second = (
            jnp.broadcast_to(table[i : i + 1, :], (GROUP, LANES)) for i in (n, n + 1)
        )
        return jnp.where(left, first, second).astype(jnp.bfloat16)

    @pl.loop(0, nodes // GROUP, unroll=2)
    def _(g):
        first = pl.multiple_of(g * GROUP, GROUP)
        span = pl.ds(first, GROUP)
        tables = [r[span, :] for r in (code_ref, low_ref, times_ref)]
        sides = []
        for eight in range(0, GROUP, EIGHT):
            marks, lows = [], []
            for n in range(eight, eight + EIGHT, 2):
                code, low, times = (pair(t, n) for t in tables)
                marks.append(
                    jnp.concatenate([jnp.where(code == r, times, zero) for r in rows], axis=0)
                )
                lows.append(
                    jnp.concatenate(
                        [jnp.where(low == r, one, zero) for r in rows[: LANES // GROUP]], axis=0
                    )
                )
            sides.append(
                lax.dot_general(
                    jnp.concatenate(marks, axis=1),
                    jnp.concatenate(lows, axis=1),
                    (((1,), (1,)), ((), ())),
                    preferred_element_type=jnp.float32,
                )
            )
        own_tile = own_tile_ref[span, :]
        hit = jnp.where(own_low_ref[span, :] == lane, one, zero)
        for t, (o, col) in enumerate(places):
            block = jnp.concatenate([side[t * EIGHT : t * EIGHT + EIGHT, :] for side in sides], axis=0)
            out_refs[o][pl.ds(counts_row + first, GROUP), col : col + LANES] = block.astype(jnp.bfloat16)
            out_refs[o][pl.ds(own_row + first, GROUP), col : col + LANES] = jnp.where(
                own_tile == jnp.bfloat16(t), hit, zero
            )


def located(ids, here):
    apart = here ^ (ids >> 8)
    same = ((apart >> 2) & 1) == 0
    dx, dz = apart & 3, (apart >> 3) & 3
    first_half = (ids & 128) == 0
    far = jnp.where(first_half, dz, dx)
    near = jnp.where(first_half, dx, dz)
    tile = jnp.where(first_half, 0, 16) + (far ^ (far >> 1)) * 4 + (near ^ (near >> 1))
    return jnp.where(same, tile, -1), ids & 127


def count_blocks(group, given, here, table, nbr, widths):
    nodes = table.shape[1]
    vmem = pl.BlockSpec(memory_space=pltpu.VMEM)
    return pl.pallas_call(
        functools.partial(count_kernel, group, len(given)),
        out_shape=[jax.ShapeDtypeStruct((4 * nodes, w), jnp.bfloat16) for w in widths],
        in_specs=[pl.BlockSpec(memory_space=pltpu.SMEM)] + [vmem] * (3 + len(given)),
        out_specs=[vmem] * len(widths),
        input_output_aliases={4 + i: i for i in range(len(given))},
        scratch_shapes=[pltpu.VMEM((LANES, LANES), jnp.float32)]
        + [pltpu.VMEM((nodes, LANES), jnp.float32)] * 3
        + [pltpu.VMEM((nodes, LANES), jnp.bfloat16)] * 2,
        compiler_params=pltpu.CompilerParams(vmem_limit_bytes=16 * 2**20),
        cost_estimate=pl.CostEstimate(
            flops=2_000_000_000, bytes_accessed=4_500_000, transcendentals=0
        ),
        name="counts",
    )(
        here,
        table[:nbr],
        table[nbr : 2 * nbr],
        table[2 * nbr].reshape(nodes // LANES, LANES),
        *given,
    )


def project_kernel(flip, here_ref, sums_ref, total_ref, self_ref, nbr_ref, out_ref):
    nodes, share = sums_ref.shape[0] // 2, sums_ref.shape[1]
    total = jnp.concatenate([total_ref[...]] * (share // LANES), axis=1)
    own = sums_ref[nodes:, :].astype(jnp.bfloat16)
    pooled = sums_ref[:nodes, :] / total
    high = pooled.astype(jnp.bfloat16)
    low = (pooled - high.astype(jnp.float32)).astype(jnp.bfloat16)
    which = (here_ref[0] & 1) ^ flip
    for part in range(2):
        first = pl.multiple_of(part * 2 * share + which * share, share)
        columns = pl.ds(first, share)
        w_self, w_nbr = self_ref[:, columns], nbr_ref[:, columns]
        out = jnp.dot(own, w_self, preferred_element_type=jnp.float32)
        out += jnp.dot(high, w_nbr, preferred_element_type=jnp.float32)
        out += jnp.dot(low, w_nbr, preferred_element_type=jnp.float32)
        out_ref[:, part * share : (part + 1) * share] = out * SCALE


def projected(flip, here, sums, total, w_self, w_neighbor):
    nodes, share = sums.shape[0] // 2, sums.shape[1]
    vmem = pl.BlockSpec(memory_space=pltpu.VMEM)
    return pl.pallas_call(
        functools.partial(project_kernel, flip),
        out_shape=jax.ShapeDtypeStruct((nodes, 2 * share), jnp.float32),
        in_specs=[pl.BlockSpec(memory_space=pltpu.SMEM)] + [vmem] * 4,
        out_specs=vmem,
        compiler_params=pltpu.CompilerParams(vmem_limit_bytes=12 * 2**20),
        cost_estimate=pl.CostEstimate(
            flops=400_000_000, bytes_accessed=4_000_000, transcendentals=0
        ),
        name="project",
    )(here, sums, total, w_self, w_neighbor)


def shards(items, self_ids, neighbor_ids, visit_counts, w_self, w_neighbor, bias):
    core, yh = lax.axis_index("core"), lax.axis_index("yh")
    batch, share = self_ids.shape[0], items.shape[1]
    nbr = neighbor_ids.shape[1]
    half = items.shape[0] // 2
    here = lax.axis_index((*DOM, "core")).reshape(1)

    axes = [("x", "z"), ("z", "x")]
    halves = [items[:half], items[half:]]
    lines, pairs = [], []
    for block, (near, _) in zip(halves, axes):
        pair = jnp.concatenate([block, moved(block, near, lambda i: i ^ 1)], axis=0)
        pairs.append(pair)
        rest = moved(pair, near, lambda i: i ^ 3)
        lines.append(jnp.concatenate([pair, rest], axis=0))
    pieces = []
    for line, (_, far) in zip(lines, axes):
        low = moved(line, far, lambda i: i ^ 1)
        high = moved(line, far, lambda i: i ^ 3)
        pieces += [line, low, high, moved(high, far, lambda i: i ^ 1)]

    table = (neighbor_ids.T, visit_counts.T, self_ids)
    kept_back, _ = lax.optimization_barrier((table, pairs))
    sent = lax.optimization_barrier(
        jnp.concatenate([kept_back[0], kept_back[1], kept_back[2][None, :]], axis=0)
    )
    theirs = moved(sent.astype(jnp.int16), "yl", lambda i: i ^ 1).astype(jnp.int32)
    table = jnp.concatenate([table[0], table[1], table[2][None, :]], axis=0)
    widths = [p.shape[0] for p in pieces]
    blocks = count_blocks(0, [], here, table, nbr, widths)
    blocks = count_blocks(1, blocks, here, theirs, nbr, widths)
    sums = sum(
        jnp.dot(blocks[i], pieces[i], preferred_element_type=jnp.float32)
        for i in (0, 4, 1, 5, 2, 6, 3, 7)
    )
    total = jnp.concatenate(
        [jnp.sum(t[nbr : 2 * nbr].astype(jnp.float32), axis=0) for t in (table, theirs)]
    )
    total = jnp.broadcast_to(total[:, None], (2 * batch, LANES))
    given = projected(1, here, sums, total, w_self, w_neighbor)
    got = moved(given.astype(jnp.float16), "core", lambda i: i ^ 1)
    kept = projected(0, here, sums, total, w_self, w_neighbor)
    chip = kept + got.astype(jnp.float32)
    first, second = chip[:, :share], chip[:, share:]
    here_part = jnp.where(yh == 0, first, second)
    there_part = jnp.where(yh == 0, second, first).astype(jnp.float16)
    from_yh = moved(there_part[:batch], "yh", lambda i: i ^ 1)
    from_yl = moved(here_part[batch:].astype(jnp.float16), "yl", lambda i: i ^ 1)
    across = lax.ppermute(there_part[batch:], ("yl", "yh"), [(i, i ^ 3) for i in range(4)])
    pre = here_part[:batch] + from_yh.astype(jnp.float32)
    pre = pre + from_yl.astype(jnp.float32) + across.astype(jnp.float32)
    my_bias = lax.dynamic_slice_in_dim(bias, (2 * yh + core) * share, share, 0)
    hidden = jnp.maximum(pre * (1.0 / SCALE) + my_bias[None, :], 0.0)
    squares = jnp.sum(hidden * hidden, axis=1)
    squares = squares + moved(squares, "core", lambda i: i ^ 1)
    squares = squares + moved(squares, "yh", lambda i: i ^ 1)
    scale = jnp.sqrt(squares / bias.shape[0] + 1e-06)[:, None]
    return hidden / scale


def solution(mesh):
    torus = Mesh(mesh.devices.reshape(4, 2, 4, 2, 2), ("z", "yl", "x", "yh", "core"))
    feat = ("yh", "core")
    placed = (
        P(DOM, feat),
        P(DOM),
        P(DOM, None),
        P(DOM, None),
        P(feat, None),
        P(feat, None),
        P(),
    )

    return jax.shard_map(
        shards, mesh=torus, in_specs=placed, out_specs=P(DOM, feat), check_vma=False
    )
```

```python
import functools

import jax
import jax.numpy as jnp
from jax import lax
from jax.experimental import pallas as pl
from jax.experimental.pallas import tpu as pltpu
from jax.sharding import Mesh
from jax.sharding import PartitionSpec as P


DOM = ("z", "yl", "x")
LANES = 128
SLOTS = 64
TILES = 32
EIGHT = 8
GROUP = 16
SCALE = 16.0


def moved(value, axis, target):
    n = lax.axis_size(axis)
    return lax.ppermute(value, axis, [(i, target(i) % n) for i in range(n)])


def count_kernel(group, n_given, here_ref, ids_ref, count_ref, self_ref, *rest):
    rest = rest[n_given:]
    out_refs, (turned, code_ref, low_ref, times_ref, own_tile_ref, own_low_ref) = rest[:-6], rest[-6:]
    nbr, nodes = ids_ref.shape
    counts_row, own_row = group * nodes, (2 + group) * nodes
    here = here_ref[0] >> 1
    places = [(o, c) for o in range(len(out_refs)) for c in range(0, out_refs[o].shape[1], LANES)]

    def column(row):
        return jnp.broadcast_to(row.astype(jnp.float32), (LANES, LANES)).T.astype(jnp.bfloat16)

    node = lax.broadcasted_iota(jnp.int32, (nbr, LANES), 1) & (EIGHT - 1)
    for part in range(nodes // LANES):
        span = pl.ds(part * LANES, LANES)
        tile, low = located(ids_ref[:, span], here)
        code = jnp.where(tile < 0, -1, tile * EIGHT + node)
        for ref, value, blank in (
            (code_ref, code, -1.0),
            (low_ref, low, -1.0),
            (times_ref, count_ref[:, span], 0.0),
        ):
            turned[...] = jnp.full((LANES, LANES), blank, jnp.float32)
            for slot in range(0, LANES, SLOTS):
                turned[slot : slot + nbr, :] = value.astype(jnp.float32)
            ref[span, :] = turned[...].T
        own_tile, own_low = located(self_ref[part : part + 1, :], here)
        own_tile_ref[span, :] = column(own_tile)
        own_low_ref[span, :] = column(own_low)

    row = lax.broadcasted_iota(jnp.int32, (GROUP, LANES), 0).astype(jnp.float32)
    rows = [(row + r * GROUP).astype(jnp.bfloat16) for r in range(TILES * EIGHT // GROUP)]
    lane = lax.broadcasted_iota(jnp.int32, (GROUP, LANES), 1)
    left = lane < SLOTS
    lane = lane.astype(jnp.float32).astype(jnp.bfloat16)
    zero = jnp.zeros((GROUP, LANES), jnp.bfloat16)
    one = jnp.ones((GROUP, LANES), jnp.bfloat16)

    def pair(table, n):
        first, second = (
            jnp.broadcast_to(table[i : i + 1, :], (GROUP, LANES)) for i in (n, n + 1)
        )
        return jnp.where(left, first, second).astype(jnp.bfloat16)

    @pl.loop(0, nodes // GROUP, unroll=2)
    def _(g):
        first = pl.multiple_of(g * GROUP, GROUP)
        span = pl.ds(first, GROUP)
        tables = [r[span, :] for r in (code_ref, low_ref, times_ref)]
        sides = []
        for eight in range(0, GROUP, EIGHT):
            marks, lows = [], []
            for n in range(eight, eight + EIGHT, 2):
                code, low, times = (pair(t, n) for t in tables)
                marks.append(
                    jnp.concatenate([jnp.where(code == r, times, zero) for r in rows], axis=0)
                )
                lows.append(
                    jnp.concatenate(
                        [jnp.where(low == r, one, zero) for r in rows[: LANES // GROUP]], axis=0
                    )
                )
            sides.append(
                lax.dot_general(
                    jnp.concatenate(marks, axis=1),
                    jnp.concatenate(lows, axis=1),
                    (((1,), (1,)), ((), ())),
                    preferred_element_type=jnp.float32,
                )
            )
        own_tile = own_tile_ref[span, :]
        hit = jnp.where(own_low_ref[span, :] == lane, one, zero)
        for t, (o, col) in enumerate(places):
            block = jnp.concatenate([side[t * EIGHT : t * EIGHT + EIGHT, :] for side in sides], axis=0)
            out_refs[o][pl.ds(counts_row + first, GROUP), col : col + LANES] = block.astype(jnp.bfloat16)
            out_refs[o][pl.ds(own_row + first, GROUP), col : col + LANES] = jnp.where(
                own_tile == jnp.bfloat16(t), hit, zero
            )


def located(ids, here):
    apart = here ^ (ids >> 8)
    same = ((apart >> 2) & 1) == 0
    dx, dz = apart & 3, (apart >> 3) & 3
    first_half = (ids & 128) == 0
    far = jnp.where(first_half, dz, dx)
    near = jnp.where(first_half, dx, dz)
    tile = jnp.where(first_half, 0, 16) + (far ^ (far >> 1)) * 4 + (near ^ (near >> 1))
    return jnp.where(same, tile, -1), ids & 127


def count_blocks(group, given, here, table, nbr, widths):
    nodes = table.shape[1]
    vmem = pl.BlockSpec(memory_space=pltpu.VMEM)
    return pl.pallas_call(
        functools.partial(count_kernel, group, len(given)),
        out_shape=[jax.ShapeDtypeStruct((4 * nodes, w), jnp.bfloat16) for w in widths],
        in_specs=[pl.BlockSpec(memory_space=pltpu.SMEM)] + [vmem] * (3 + len(given)),
        out_specs=[vmem] * len(widths),
        input_output_aliases={4 + i: i for i in range(len(given))},
        scratch_shapes=[pltpu.VMEM((LANES, LANES), jnp.float32)]
        + [pltpu.VMEM((nodes, LANES), jnp.float32)] * 3
        + [pltpu.VMEM((nodes, LANES), jnp.bfloat16)] * 2,
        compiler_params=pltpu.CompilerParams(vmem_limit_bytes=16 * 2**20),
        cost_estimate=pl.CostEstimate(
            flops=2_000_000_000, bytes_accessed=4_500_000, transcendentals=0
        ),
        name="counts",
    )(
        here,
        table[:nbr],
        table[nbr : 2 * nbr],
        table[2 * nbr].reshape(nodes // LANES, LANES),
        *given,
    )


def project_kernel(flip, here_ref, sums_ref, total_ref, weights_ref, out_ref):
    nodes, share = sums_ref.shape[0] // 2, sums_ref.shape[1]
    total = jnp.concatenate([total_ref[...]] * (share // LANES), axis=1)
    own = sums_ref[nodes:, :].astype(jnp.bfloat16)
    pooled = sums_ref[:nodes, :] / total
    high = pooled.astype(jnp.bfloat16)
    low = (pooled - high.astype(jnp.float32)).astype(jnp.bfloat16)
    which = (here_ref[0] & 1) ^ flip
    for part in range(2):
        first = pl.multiple_of(part * 2 * share + which * share, share)
        columns = pl.ds(first, share)
        w_self, w_nbr = weights_ref[:share, columns], weights_ref[share:, columns]
        out = jnp.dot(own, w_self, preferred_element_type=jnp.float32)
        out += jnp.dot(high, w_nbr, preferred_element_type=jnp.float32)
        out += jnp.dot(low, w_nbr, preferred_element_type=jnp.float32)
        out_ref[:, part * share : (part + 1) * share] = out * SCALE


def projected(flip, here, sums, total, weights):
    nodes, share = sums.shape[0] // 2, sums.shape[1]
    vmem = pl.BlockSpec(memory_space=pltpu.VMEM)
    return pl.pallas_call(
        functools.partial(project_kernel, flip),
        out_shape=jax.ShapeDtypeStruct((nodes, 2 * share), jnp.float32),
        in_specs=[pl.BlockSpec(memory_space=pltpu.SMEM)] + [vmem] * 3,
        out_specs=vmem,
        compiler_params=pltpu.CompilerParams(vmem_limit_bytes=12 * 2**20),
        cost_estimate=pl.CostEstimate(
            flops=400_000_000, bytes_accessed=4_000_000, transcendentals=0
        ),
        name="project",
    )(here, sums, total, weights)


def shards(items, self_ids, neighbor_ids, visit_counts, w_self, w_neighbor, bias):
    core, yh = lax.axis_index("core"), lax.axis_index("yh")
    batch, share = self_ids.shape[0], items.shape[1]
    nbr = neighbor_ids.shape[1]
    half = items.shape[0] // 2
    here = lax.axis_index((*DOM, "core")).reshape(1)

    axes = [("x", "z"), ("z", "x")]
    halves = [items[:half], items[half:]]
    lines, pairs = [], []
    for block, (near, _) in zip(halves, axes):
        pair = jnp.concatenate([block, moved(block, near, lambda i: i ^ 1)], axis=0)
        pairs.append(pair)
        rest = moved(pair, near, lambda i: i ^ 3)
        lines.append(jnp.concatenate([pair, rest], axis=0))
    pieces = []
    for line, (_, far) in zip(lines, axes):
        low = moved(line, far, lambda i: i ^ 1)
        high = moved(line, far, lambda i: i ^ 3)
        pieces += [line, low, high, moved(high, far, lambda i: i ^ 1)]

    table = (neighbor_ids.T, visit_counts.T, self_ids)
    kept_back, _ = lax.optimization_barrier((table, pairs))
    sent = lax.optimization_barrier(
        jnp.concatenate([kept_back[0], kept_back[1], kept_back[2][None, :]], axis=0)
    )
    theirs = moved(sent.astype(jnp.int16), "yl", lambda i: i ^ 1).astype(jnp.int32)
    table = jnp.concatenate([table[0], table[1], table[2][None, :]], axis=0)
    weights = jnp.concatenate([w_self, w_neighbor], axis=0)
    widths = [p.shape[0] for p in pieces]
    blocks = count_blocks(0, [], here, table, nbr, widths)
    blocks = count_blocks(1, blocks, here, theirs, nbr, widths)
    sums = sum(
        jnp.dot(blocks[i], pieces[i], preferred_element_type=jnp.float32)
        for i in (0, 4, 1, 5, 2, 6, 3, 7)
    )
    total = jnp.concatenate(
        [jnp.sum(t[nbr : 2 * nbr].astype(jnp.float32), axis=0) for t in (table, theirs)]
    )
    total = jnp.broadcast_to(total[:, None], (2 * batch, LANES))
    given = projected(1, here, sums, total, weights)
    got = moved(given.astype(jnp.float16), "core", lambda i: i ^ 1)
    kept = projected(0, here, sums, total, weights)
    chip = kept + got.astype(jnp.float32)
    first, second = chip[:, :share], chip[:, share:]
    here_part = jnp.where(yh == 0, first, second)
    there_part = jnp.where(yh == 0, second, first).astype(jnp.float16)
    from_yh = moved(there_part[:batch], "yh", lambda i: i ^ 1)
    from_yl = moved(here_part[batch:].astype(jnp.float16), "yl", lambda i: i ^ 1)
    across = lax.ppermute(there_part[batch:], ("yl", "yh"), [(i, i ^ 3) for i in range(4)])
    pre = here_part[:batch] + from_yh.astype(jnp.float32)
    pre = pre + from_yl.astype(jnp.float32) + across.astype(jnp.float32)
    my_bias = lax.dynamic_slice_in_dim(bias, (2 * yh + core) * share, share, 0)
    hidden = jnp.maximum(pre * (1.0 / SCALE) + my_bias[None, :], 0.0)
    squares = jnp.sum(hidden * hidden, axis=1)
    squares = squares + moved(squares, "core", lambda i: i ^ 1)
    squares = squares + moved(squares, "yh", lambda i: i ^ 1)
    scale = jnp.sqrt(squares / bias.shape[0] + 1e-06)[:, None]
    return hidden / scale


def solution(mesh):
    torus = Mesh(mesh.devices.reshape(4, 2, 4, 2, 2), ("z", "yl", "x", "yh", "core"))
    feat = ("yh", "core")
    placed = (
        P(DOM, feat),
        P(DOM),
        P(DOM, None),
        P(DOM, None),
        P(feat, None),
        P(feat, None),
        P(),
    )

    return jax.shard_map(
        shards, mesh=torus, in_specs=placed, out_specs=P(DOM, feat), check_vma=False
    )
```
